32 devices in a mesh: parts: 2 (over y), rows: 4 (over x, core), cols: 4 (over z).
Axes of the slice: x: 2, y: 2, z: 4, core: 2. Of those that a mesh axis runs over, the one named last changes fastest.
Arguments:
- pair: float32 [256, 4, 32, 128], P(('parts', 'rows'), None, 'cols'), parts along dimension 0, may hold values from -6 to 6
- singles: float32 [256, 384], P(('parts', 'rows')), parts along dimension 0, may hold values from -6 to 6
- restype: int32 [256], P(('parts', 'rows')), parts along dimension 0, may hold values from 0 to 31
- block_mask: int32 [32, 4, 4], P(('parts', 'rows'), None, 'cols'), parts along dimension 0, may hold values from 0 to 1, as said below
- ln_trans: float32 [128], replicated, may hold values from 0.1 to 1.9
- w_trans_in: bfloat16 [128, 1024], replicated, may hold values from -0.5 to 0.5
- w_trans_out: bfloat16 [512, 128], replicated, may hold values from -0.25 to 0.25
- ln_bias: float32 [128], replicated, may hold values from 0.1 to 1.9
- w_bias: bfloat16 [128, 16], replicated, may hold values from -0.5 to 0.5
- restype_table: float32 [32, 384], replicated, may hold values from -6 to 6
- ln_single: float32 [384], replicated, may hold values from 0.1 to 1.9
- w_attn: bfloat16 [384, 1536], replicated, may hold values from -80 to 80
- w_single_out: bfloat16 [384, 384], replicated, may hold values from -0.3125 to 0.3125
- w_dist: bfloat16 [128, 64], replicated, may hold values from -0.5 to 0.5
- dist_bias: float32 [64], replicated, may hold values from -6 to 6
Outputs:
- pair_next: float32 [256, 4, 32, 128], P(('parts', 'rows'), None, 'cols'), parts along dimension 0
- singles_next: float32 [256, 384], P(('parts', 'rows')), parts along dimension 0
- dist_logits: float32 [256, 4, 2048], P(('parts', 'rows'), None, 'cols'), parts along dimension 0
The draws below stay inside these ranges and needn't reach their ends.
There are 2 independent parts, one for each index of `parts`. The reference program is written for one: setup_inputs(seed, part) draws one part's arguments, and reference() takes and returns one part's arrays. A program takes and returns all parts, laid end to end along the dimension named above; an argument that names none is the same for every part. Nothing has to cross between parts.
Inputs may be any that keep to these rules, and one draw needn't show every extreme that they name: block_mask[p, a, c] is 1 where p == a * 4 + c.
All inputs are finite; a program needn't handle non-finite values.
Results may differ from the reference program's by a relative error of at most 0.0044.
Values may be sent and summed in bfloat16 or wider, within the bound.
No kernel may reach another device: no remote copies, remote signals or barrier semaphores. Data moves between devices by JAX's collectives and lax.ppermute only.
A program may use at most 64 MiB of HBM per device.

```python
import math
import jax
import jax.numpy as jnp
from jax import lax

C_PAIR = 128
TRANS = 512
C_SINGLE = 384
HEADS = 16
HEAD_DIM = 24
BINS = 64
RESTYPES = 32
BLK = 8
NBLK = 16
N = 128
N_ROWS = 4
N_COLS = 4


def draw_block_mask(key, part):
    picks = jax.random.randint(key, (NBLK, NBLK), 0, 4)
    diagonal = jnp.arange(NBLK, dtype=jnp.int32)[:, None] == jnp.arange(NBLK, dtype=jnp.int32)[None, :]
    allowed = jnp.logical_or(picks > 0, diagonal).astype(jnp.int32)
    return allowed.reshape(NBLK, N_ROWS, N_COLS)


def draw_w_attn(key, part):
    base = jax.random.truncated_normal(key, -4.0, 4.0, (C_SINGLE, 4 * C_SINGLE), jnp.float32) / math.sqrt(C_SINGLE)
    return base.astype(jnp.bfloat16)


def set_ends(drawn, stream_key, low, top_value):
    shape = drawn.shape
    spot = [jax.random.randint(jax.random.fold_in(stream_key, axis), (), 0, shape[axis]) for axis in range(len(shape))]
    drawn = drawn.at[tuple(spot)].set(low)
    longest = shape.index(max(shape))
    spot[longest] = (spot[longest] + 1) % shape[longest]
    return drawn.at[tuple(spot)].set(top_value)


def steps_of(own_key, shape, split, smallest, high):
    level = 1.0
    for dim, shards_of in split:
        steps = jax.random.uniform(jax.random.fold_in(jax.random.fold_in(own_key, 6), dim), (shards_of,), jnp.float32, smallest / len(split), high / len(split))
        level = level * jnp.repeat(jnp.exp(steps), shape[dim] // shards_of).reshape((-1,) + (1,) * (len(shape) - 1 - dim))
    return level


def scatter_about(rng, dims, width, limit, pieces=(), kind=jnp.bfloat16):
    factor_of = steps_of(rng, dims, pieces, -0.22, 0.18) if pieces else 1.0
    array = jax.random.normal(rng, dims, jnp.float32) * width * factor_of
    return jnp.minimum(jnp.maximum(array, -limit), limit).astype(kind)


def setup_inputs(seed: int = 0, part: int = 0) -> dict:
    keys = jax.random.split(jax.random.key(seed), 16)
    part_keys = jax.random.split(jax.random.fold_in(keys[15], part), 16)
    pair = scatter_about(part_keys[0], (N, N_ROWS, N_COLS * BLK, C_PAIR), 1.0, 6.0, ((0, 4), (2, 4)), jnp.float32)
    singles = scatter_about(part_keys[1], (N, C_SINGLE), 1.0, 6.0, ((0, 4),), jnp.float32)
    restype = set_ends(jax.random.randint(part_keys[2], (N,), 0, RESTYPES), jax.random.fold_in(part_keys[2], 1), 0, RESTYPES - 1).astype(jnp.int32)
    block_mask = draw_block_mask(jax.random.fold_in(jax.random.fold_in(keys[15], part), 71), part)
    ln_trans = jnp.clip(1.0 + 0.18 * jax.random.normal(keys[4], (C_PAIR,), jnp.float32), 0.1, 1.9)
    w_trans_in = scatter_about(keys[5], (C_PAIR, 2 * TRANS), C_PAIR ** -0.5, 0.5)
    w_trans_out = scatter_about(keys[6], (TRANS, C_PAIR), TRANS ** -0.5, 0.25)
    ln_bias = jnp.clip(1.0 + 0.18 * jax.random.normal(keys[7], (C_PAIR,), jnp.float32), 0.1, 1.9)
    w_bias = scatter_about(keys[8], (C_PAIR, HEADS), C_PAIR ** -0.5, 0.5)
    restype_table = scatter_about(keys[9], (RESTYPES, C_SINGLE), 1.0, 6.0, (), jnp.float32)
    ln_single = jnp.clip(1.0 + 0.18 * jax.random.normal(keys[10], (C_SINGLE,), jnp.float32), 0.1, 1.9)
    w_attn = draw_w_attn(jax.random.fold_in(keys[15], 71), part)
    w_single_out = scatter_about(keys[12], (C_SINGLE, C_SINGLE), C_SINGLE ** -0.5, 0.3125)
    w_dist = scatter_about(keys[13], (C_PAIR, BINS), C_PAIR ** -0.5, 0.5)
    dist_bias = scatter_about(keys[14], (BINS,), 1.0, 6.0, (), jnp.float32)
    return dict(pair=pair, singles=singles, restype=restype, block_mask=block_mask, ln_trans=ln_trans, w_trans_in=w_trans_in, w_trans_out=w_trans_out, ln_bias=ln_bias, w_bias=w_bias, restype_table=restype_table, ln_single=ln_single, w_attn=w_attn, w_single_out=w_single_out, w_dist=w_dist, dist_bias=dist_bias)


eps_norm = 1e-05

def layer_norm(values, gain_vec):
    average = lax.optimization_barrier(jnp.mean(values, axis=-1, keepdims=True))
    centred = values - average
    spread = lax.optimization_barrier(jnp.mean(centred * centred, axis=-1, keepdims=True))
    return centred * lax.rsqrt(spread + eps_norm) * gain_vec

def pair_block(pair_rows, ln_trans, w_trans_in, w_trans_out, ln_bias, w_bias, w_dist):
    hidden_units = w_trans_out.shape[0]
    normed = layer_norm(pair_rows, ln_trans).astype(jnp.bfloat16)
    gate_up = jnp.dot(normed, w_trans_in, preferred_element_type=jnp.float32)
    hidden = (jax.nn.silu(gate_up[:, :hidden_units]) * gate_up[:, hidden_units:]).astype(jnp.bfloat16)
    updated = pair_rows + jnp.dot(hidden, w_trans_out, preferred_element_type=jnp.float32)
    biased = layer_norm(updated, ln_bias).astype(jnp.bfloat16)
    head_bias = jnp.dot(biased, w_bias, preferred_element_type=jnp.float32)
    binned = jnp.dot(updated.astype(jnp.bfloat16), w_dist, preferred_element_type=jnp.float32).astype(jnp.bfloat16)
    return (updated, head_bias, binned)

def widen(values):
    return lax.optimization_barrier(values).astype(jnp.float32)

def reference(pair, singles, restype, block_mask, ln_trans, w_trans_in, w_trans_out, ln_bias, w_bias, restype_table, ln_single, w_attn, w_single_out, w_dist, dist_bias):
    flat = pair.reshape(N, N, C_PAIR)
    rows_step = math.gcd(N, 64)
    pair_tiles = flat.reshape(N // rows_step, rows_step * N, C_PAIR)

    def run_tile(pair_tile):
        return pair_block(pair_tile, ln_trans, w_trans_in, w_trans_out, ln_bias, w_bias, w_dist)
    updated, head_bias, binned = lax.map(run_tile, pair_tiles)
    updated = updated.reshape(N, N, C_PAIR)
    head_bias = head_bias.reshape(N, N, HEADS)
    binned = binned.reshape(N, N, BINS)
    one_hot = (restype[:, None] == jnp.arange(RESTYPES, dtype=jnp.int32)[None, :]).astype(jnp.float32)
    embedded = singles + jnp.dot(one_hot, restype_table, precision=lax.Precision.HIGHEST)
    normed_s = layer_norm(embedded, ln_single).astype(jnp.bfloat16)
    query_proj = (jnp.dot(normed_s, w_attn[:, :C_SINGLE], preferred_element_type=jnp.float32) * HEAD_DIM ** (-0.5)).astype(jnp.bfloat16)
    key_proj = jnp.dot(normed_s, w_attn[:, C_SINGLE:2 * C_SINGLE], preferred_element_type=jnp.float32).astype(jnp.bfloat16)
    value_proj = jnp.dot(normed_s, w_attn[:, 2 * C_SINGLE:3 * C_SINGLE], preferred_element_type=jnp.float32).astype(jnp.bfloat16)
    gate_vals = jax.nn.sigmoid(jnp.dot(normed_s, w_attn[:, 3 * C_SINGLE:], preferred_element_type=jnp.float32))
    q_heads = widen(query_proj).reshape(N, HEADS, HEAD_DIM)
    k_heads = widen(key_proj).reshape(N, HEADS, HEAD_DIM)
    v_heads = widen(value_proj).reshape(N, HEADS, HEAD_DIM)
    scores = jnp.einsum('qhd,khd->hqk', q_heads, k_heads) + jnp.transpose(head_bias, (2, 0, 1))
    block_full = block_mask.reshape(NBLK, NBLK)
    allowed = jnp.repeat(jnp.repeat(block_full, BLK, axis=0), BLK, axis=1) > 0
    scores = jnp.where(allowed[None], scores, jnp.float32(-1000000000.0))
    row_max = lax.optimization_barrier(jnp.max(scores, axis=-1))
    expo = jnp.exp(scores - row_max[:, :, None])
    totals = lax.optimization_barrier(jnp.sum(expo, axis=-1))
    weighted = jnp.einsum('hqk,khd->qhd', widen(expo.astype(jnp.bfloat16)), v_heads)
    normalised = weighted / jnp.transpose(totals)[:, :, None]
    attended = (gate_vals * normalised.reshape(N, C_SINGLE)).astype(jnp.bfloat16)
    singles_next = embedded + jnp.dot(attended, w_single_out, preferred_element_type=jnp.float32)
    logits = binned.astype(jnp.float32) + jnp.transpose(binned, (1, 0, 2)).astype(jnp.float32) + dist_bias
    dist_logits = logits.reshape(N, N_ROWS, N_COLS * BLK * BINS)
    pair_next = updated.reshape(N, N_ROWS, N_COLS * BLK, C_PAIR)
    return (pair_next, singles_next, dist_logits)
```

```python
import functools

import jax
import jax.numpy as jnp
from jax import lax
from jax.experimental import pallas as pl
from jax.experimental.pallas import tpu as pltpu
from jax.sharding import PartitionSpec as P

EPS = 1e-05
MASKED = -1000000000.0
F32, BF16 = jnp.float32, jnp.bfloat16
NT = (((1,), (1,)), ((), ()))
TN = (((0,), (0,)), ((), ()))


def layer_norm(values, gain_vec):
    average = jnp.mean(values, axis=-1, keepdims=True)
    centred = values - average
    spread = jnp.mean(centred * centred, axis=-1, keepdims=True)
    return centred * lax.rsqrt(spread + EPS) * gain_vec


def sigmoid(values):
    return 0.5 + 0.5 * jnp.tanh(0.5 * values)


def head_mask(heads, width):
    size = width // heads
    first = lax.broadcasted_iota(jnp.int32, (heads, width), 0) * size
    column = lax.broadcasted_iota(jnp.int32, (heads, width), 1)
    return jnp.logical_and(column >= first, column < first + size)


def doubled(w_t):
    zero = jnp.zeros_like(w_t)
    return jnp.concatenate(
        [jnp.concatenate([w_t, zero], 1), jnp.concatenate([zero, w_t], 1)], 0
    )


def transition_kernel(
    n_rows,
    pair_ref, ln_trans_ref, w_in_ref, w_out_ref, w_dist_ref,
    singles_ref, restype_ref, table_ref, ln_single_ref,
    next_ref, emb_ref, y_ref, *rest,
):
    out_refs, (proj_s, y_s) = rest[:n_rows], rest[n_rows:]
    row, col = lax.axis_index("rows"), lax.axis_index("cols")
    blocks, _, groups, length, lanes = proj_s.shape
    keys = groups * length
    width = singles_ref.shape[1]
    types = lax.broadcasted_iota(jnp.int32, (table_ref.shape[0], restype_ref.shape[1]), 0)
    one_hot = (types == restype_ref[...]).astype(F32)
    emb = singles_ref[...] + lax.dot_general(
        one_hot, table_ref[...], TN, precision=lax.Precision.HIGHEST, preferred_element_type=F32
    )
    emb_ref[...] = emb
    y = layer_norm(emb, ln_single_ref[...])
    y_ref[...] = y.astype(BF16)
    y_s[...] = y.reshape(y_s.shape)
    y_own = y_s[col].astype(BF16)
    hidden = w_out_ref.shape[0]
    tile = length * keys
    w_dist2 = doubled(w_dist_ref[...])
    for b in range(blocks):
        z = pair_ref[b * tile : (b + 1) * tile, :]
        xt = layer_norm(z, ln_trans_ref[...]).astype(BF16)
        gu = jnp.dot(xt, w_in_ref[...], preferred_element_type=F32)
        gate, up = gu[:, :hidden], gu[:, hidden:]
        hid = (gate * sigmoid(gate) * up).astype(BF16)
        new = z + jnp.dot(hid, w_out_ref[...], preferred_element_type=F32)
        next_ref[b * tile : (b + 1) * tile, :] = new
        low = new.astype(BF16)
        pairs = [
            jnp.concatenate(
                [low[t * keys : (t + 1) * keys], low[(t + 1) * keys : (t + 2) * keys]], 1
            )
            for t in range(0, length, 2)
        ]
        proj = lax.dot_general(jnp.concatenate(pairs, 0), w_dist2, NT, preferred_element_type=F32)
        proj_s[b] = proj.reshape(length // 2, groups, length, lanes)
    for k in range(n_rows):
        to = row ^ k
        for b in range(blocks):
            for t in range(length // 2):
                out_refs[k][b, :, t * lanes : (t + 1) * lanes] = proj_s[b, t, to].astype(BF16)
        out_refs[k][blocks, :, :width] = y_own
        out_refs[k][blocks, :, width:] = jnp.zeros(
            (length, out_refs[k].shape[2] - width), BF16
        )


def own_kernel(
    next_ref, ln_bias_ref, w_bias_ref, w_dist_ref, dist_bias_ref, y_ref, w_attn_ref, mask_ref,
    bias_ref, own_ref, q_ref, gate_ref, keep_ref,
):
    heads, channels = w_bias_ref.shape
    groups, blocks, length, wide = own_ref.shape
    keys, queries = groups * length, blocks * length
    width = y_ref.shape[1]
    lanes = length * heads
    tiled = jnp.concatenate([w_bias_ref[...]] * length, 0)
    owner = lax.broadcasted_iota(jnp.int32, tiled.shape, 0) // heads
    w_big = jnp.concatenate(
        [jnp.where(owner == t, tiled, jnp.zeros_like(tiled)) for t in range(length)], 1
    )
    rows = []
    for b in range(blocks):
        new = next_ref[b * length * keys : (b + 1) * length * keys, :]
        xb = layer_norm(new, ln_bias_ref[...]).astype(BF16)
        rows.append(
            jnp.concatenate([xb[t * keys : (t + 1) * keys] for t in range(length)], 1)
        )
    bias = lax.dot_general(jnp.concatenate(rows, 0), w_big, NT, preferred_element_type=F32)
    for b in range(blocks):
        bias_ref[:, b * lanes : (b + 1) * lanes] = bias[b * keys : (b + 1) * keys]
    bins = w_dist_ref.shape[0]
    w_dist2 = doubled(w_dist_ref[...])
    both = jnp.concatenate([dist_bias_ref[...]] * 2, 1)
    for a in range(groups):
        picked = []
        for t in range(0, length, 2):
            halves = [
                next_ref[pl.ds(a * length + t + s, queries, stride=keys), :].astype(BF16)
                for s in range(2)
            ]
            picked.append(jnp.concatenate(halves, 1))
        proj = lax.dot_general(jnp.concatenate(picked, 0), w_dist2, NT, preferred_element_type=F32)
        proj = proj.astype(BF16).astype(F32) + both
        for t in range(length // 2):
            own_ref[a, :, :, t * 2 * bins : (t + 1) * 2 * bins] = proj[
                t * queries : (t + 1) * queries
            ].reshape(blocks, length, 2 * bins)
    size = width // heads
    y = y_ref[...]
    q = jnp.dot(y, w_attn_ref[:, :width], preferred_element_type=F32) * size ** (-0.5)
    q_ref[...] = q.astype(BF16)
    gate_ref[...] = sigmoid(
        jnp.dot(y, w_attn_ref[:, 3 * width :], preferred_element_type=F32)
    )
    for a in range(groups):
        for b in range(blocks):
            keep_ref[a * length : (a + 1) * length, b * lanes : (b + 1) * lanes] = jnp.full(
                (length, lanes), mask_ref[b * groups + a], jnp.int32
            )


def attention_kernel(n_rows, n_cols, heads, q_ref, bias_ref, keep_ref, w_attn_ref, *rest):
    got_refs, out_refs, y_s = rest[:n_rows], rest[n_rows:-1], rest[-1]
    row, col = lax.axis_index("rows"), lax.axis_index("cols")
    groups, length, width = y_s.shape
    queries = q_ref.shape[0]
    blocks = queries // length
    keys = groups * length
    for k in range(n_rows):
        y_s[row ^ k] = got_refs[k][blocks, :, :width].astype(F32)
    y = y_s[...].reshape(keys, width).astype(BF16)
    kv = jnp.dot(y, w_attn_ref[:, width : 3 * width], preferred_element_type=F32).astype(BF16)
    mine = head_mask(heads, width)
    spread = jnp.where(mine[None], q_ref[...].astype(F32)[:, None, :], 0.0)
    spread = spread.reshape(queries * heads, width).astype(BF16)
    scores = lax.dot_general(kv[:, :width], spread, NT, preferred_element_type=F32)
    scores = jnp.where(keep_ref[...] > 0, scores + bias_ref[...], MASKED)
    top = jnp.max(scores, axis=0, keepdims=True)
    expo = jnp.exp(scores - top)
    total = jnp.sum(expo, axis=0, keepdims=True)
    acc = lax.dot_general(expo.astype(BF16), kv[:, width:], TN, preferred_element_type=F32)
    acc = jnp.sum(
        jnp.where(mine[None], acc.reshape(queries, heads, width), 0.0), axis=1
    )
    t0 = top.astype(BF16)
    t1 = (top - t0.astype(F32)).astype(BF16)
    t2 = (top - t0.astype(F32) - t1.astype(F32)).astype(BF16)
    s0 = total.astype(BF16)
    s1 = (total - s0.astype(F32)).astype(BF16)
    stats = jnp.concatenate([v.astype(F32) for v in (t0, t1, t2, s0, s1)], 0)
    stats = jnp.concatenate([stats, jnp.zeros((3, stats.shape[1]), F32)], 0).astype(BF16)
    room = out_refs[0].shape[2] - width
    piece = lax.broadcasted_iota(jnp.int32, (8, room), 0)
    lane = lax.broadcasted_iota(jnp.int32, (8, room), 1)
    place = (lane // heads == piece).astype(BF16)
    stats = lax.dot_general(stats, place, TN, preferred_element_type=F32)
    head = lax.broadcasted_iota(jnp.int32, (heads, room), 0)
    lane = lax.broadcasted_iota(jnp.int32, (heads, room), 1)
    stats = jnp.sum(
        jnp.where((lane % heads == head)[None], stats.reshape(queries, heads, room), 0.0), axis=1
    )
    part = jnp.concatenate([acc, stats], 1).reshape(blocks, length, width + room).astype(BF16)
    for k in range(n_cols):
        to = col ^ k
        for j in range(n_rows):
            out_refs[k][j] = got_refs[j][to]
        out_refs[k][n_rows:] = part


def tree_sum(values):
    while len(values) > 1:
        values = [values[i] + values[i + 1] for i in range(0, len(values), 2)]
    return values[0]


def final_kernel(
    n_rows, n_cols, heads, own_ref, emb_ref, gate_ref, w_out_ref, *rest
):
    got_refs, singles_ref, logits_ref = rest[:n_cols], rest[n_cols], rest[n_cols + 1]
    row, col = lax.axis_index("rows"), lax.axis_index("cols")
    groups, blocks, length, wide = own_ref.shape
    queries, width = emb_ref.shape
    for k in range(n_cols):
        source = col ^ k
        for a in range(groups):
            logits_ref[pl.ds(source * length, length), a, :] = (
                own_ref[a, source] + got_refs[k][row ^ a].astype(F32)
            )
    tops, sums, accs = [], [], []
    for k in range(n_cols):
        part = got_refs[k][n_rows:].astype(F32).reshape(queries, wide)
        accs.append(part[:, :width])
        piece = [part[:, width + heads * p : width + heads * (p + 1)] for p in range(5)]
        tops.append(piece[0] + piece[1] + piece[2])
        sums.append(piece[3] + piece[4])
    top = functools.reduce(jnp.maximum, tops)
    scale = [jnp.exp(t - top) for t in tops]
    total = tree_sum([s * w for s, w in zip(sums, scale)])
    share = jnp.concatenate([w / total for w in scale], 0)
    share = jnp.dot(
        share,
        head_mask(heads, width).astype(F32),
        precision=lax.Precision.HIGHEST,
        preferred_element_type=F32,
    )
    mixed = tree_sum([
        acc * share[k * queries : (k + 1) * queries] for k, acc in enumerate(accs)
    ])
    att = (gate_ref[...] * mixed).astype(BF16)
    singles_ref[...] = emb_ref[...] + jnp.dot(att, w_out_ref[...], preferred_element_type=F32)


def call(kernel, name, outs, scratch, flops, limit, smem, *args):
    shapes = [jax.ShapeDtypeStruct(s, d) for s, d in outs]
    touched = sum(a.size * a.dtype.itemsize for a in (*args, *shapes))
    spec = pl.BlockSpec(memory_space=pltpu.VMEM)
    return pl.pallas_call(
        kernel,
        name=name,
        out_shape=shapes,
        in_specs=[
            pl.BlockSpec(memory_space=pltpu.SMEM) if i in smem else spec for i in range(len(args))
        ],
        out_specs=[spec] * len(shapes),
        scratch_shapes=scratch,
        cost_estimate=pl.CostEstimate(flops=flops, bytes_accessed=touched, transcendentals=0),
        compiler_params=pltpu.CompilerParams(vmem_limit_bytes=limit),
    )(*args)


def local(
    n_rows, n_cols,
    pair, singles, restype, block_mask, ln_trans, w_trans_in, w_trans_out, ln_bias, w_bias,
    restype_table, ln_single, w_attn, w_single_out, w_dist, dist_bias,
):
    queries, groups, length, channels = pair.shape
    keys = groups * length
    blocks = queries // length
    heads = w_bias.shape[1]
    width = w_single_out.shape[0]
    bins = w_dist.shape[1]
    hidden = w_trans_out.shape[0]
    wide = length * bins
    rows = queries * keys
    mib = 1 << 20
    room = (16 if rows <= 2048 else 40) * mib
    first = call(
        functools.partial(transition_kernel, n_rows),
        "transition",
        [((rows, channels), F32), ((queries, width), F32), ((queries, width), BF16)]
        + [((blocks + 1, length, wide), BF16)] * n_rows,
        [
            pltpu.VMEM((blocks, length // 2, groups, length, 2 * bins), F32),
            pltpu.VMEM((blocks, length, width), F32),
        ],
        2 * rows * channels * hidden * 3,
        room,
        (),
        pair.reshape(rows, channels), ln_trans[None], w_trans_in, w_trans_out, w_dist.T,
        singles, restype[None], restype_table, ln_single[None],
    )
    pair_next, emb, y, *blocks_out = first
    got = [blocks_out[0]] + [
        lax.ppermute(blocks_out[k], "rows", [(i, i ^ k) for i in range(n_rows)])
        for k in range(1, n_rows)
    ]
    bias, own, q, gate, keep = call(
        own_kernel,
        "own",
        [
            ((keys, queries * heads), F32),
            ((groups, blocks, length, wide), F32),
            ((queries, width), BF16),
            ((queries, width), F32),
            ((keys, queries * heads), jnp.int32),
        ],
        [],
        2 * rows * channels * 1024,
        room,
        (7,),
        pair_next, ln_bias[None], w_bias.T, w_dist.T, dist_bias[None], y, w_attn,
        block_mask.reshape(blocks * groups),
    )
    parts = call(
        functools.partial(attention_kernel, n_rows, n_cols, heads),
        "attention",
        [((groups + blocks, length, wide), BF16)] * n_cols,
        [pltpu.VMEM((groups, length, width), F32)],
        2 * rows * channels * 256,
        room,
        (),
        q, bias, keep, w_attn, *got,
    )
    mixed = [parts[0]] + [
        lax.ppermute(parts[k], "cols", [(i, i ^ k) for i in range(n_cols)])
        for k in range(1, n_cols)
    ]
    singles_next, dist_logits = call(
        functools.partial(final_kernel, n_rows, n_cols, heads),
        "final",
        [((queries, width), F32), ((queries, groups, wide), F32)],
        [],
        2 * rows * channels * 128,
        room,
        (),
        own, emb, gate, w_single_out, *mixed,
    )
    return pair_next.reshape(pair.shape), singles_next, dist_logits


def solution(mesh):
    return jax.shard_map(
        functools.partial(local, mesh.shape["rows"], mesh.shape["cols"]),
        mesh=mesh,
        in_specs=(
            P(("parts", "rows"), None, "cols", None),
            P(("parts", "rows"), None),
            P(("parts", "rows")),
            P(("parts", "rows"), None, "cols"),
            *([P()] * 11),
        ),
        out_specs=(
            P(("parts", "rows"), None, "cols", None),
            P(("parts", "rows"), None),
            P(("parts", "rows"), None, "cols"),
        ),
        check_vma=False,
    )
```

```python
import functools

import jax
import jax.numpy as jnp
from jax import lax
from jax.experimental import pallas as pl
from jax.experimental.pallas import tpu as pltpu
from jax.sharding import PartitionSpec as P

EPS = 1e-05
MASKED = -1000000000.0
F32, BF16 = jnp.float32, jnp.bfloat16
NT = (((1,), (1,)), ((), ()))
TN = (((0,), (0,)), ((), ()))


def layer_norm(values, gain_vec):
    average = jnp.mean(values, axis=-1, keepdims=True)
    centred = values - average
    spread = jnp.mean(centred * centred, axis=-1, keepdims=True)
    return centred * lax.rsqrt(spread + EPS) * gain_vec


def sigmoid(values):
    return 0.5 + 0.5 * jnp.tanh(0.5 * values)


def head_mask(heads, width):
    size = width // heads
    first = lax.broadcasted_iota(jnp.int32, (heads, width), 0) * size
    column = lax.broadcasted_iota(jnp.int32, (heads, width), 1)
    return jnp.logical_and(column >= first, column < first + size)


def doubled(w_t):
    zero = jnp.zeros_like(w_t)
    return jnp.concatenate(
        [jnp.concatenate([w_t, zero], 1), jnp.concatenate([zero, w_t], 1)], 0
    )


def transition_kernel(
    n_rows,
    pair_hbm, ln_trans_hbm, w_in_hbm, w_out_hbm, w_dist_hbm,
    singles_hbm, restype_hbm, table_hbm, ln_single_hbm,
    next_ref, emb_ref, y_ref, *rest,
):
    out_refs, rest = rest[:n_rows], rest[n_rows:]
    (proj_s, y_s, pair_s, ln_trans_s, w_in_s, w_out_s, w_dist_s,
     singles_s, restype_s, table_s, ln_single_s, sems) = rest
    blocks, _, groups, length, lanes = proj_s.shape
    keys = groups * length
    tile = length * keys
    moves = [
        pltpu.make_async_copy(source, target, sems.at[i])
        for i, (source, target) in enumerate((
            (restype_hbm, restype_s), (table_hbm, table_s), (singles_hbm, singles_s),
            (ln_single_hbm, ln_single_s), (ln_trans_hbm, ln_trans_s), (w_in_hbm, w_in_s),
            (w_out_hbm, w_out_s), (w_dist_hbm, w_dist_s), (pair_hbm, pair_s),
        ))
    ]
    for move in moves:
        move.start()
    for move in moves:
        move.wait()
    row, col = lax.axis_index("rows"), lax.axis_index("cols")
    width = singles_s.shape[1]
    types = lax.broadcasted_iota(jnp.int32, (table_s.shape[0], restype_s.shape[1]), 0)
    one_hot = (types == restype_s[...]).astype(F32)
    emb = singles_s[...] + lax.dot_general(
        one_hot, table_s[...], TN, precision=lax.Precision.HIGHEST, preferred_element_type=F32
    )
    emb_ref[...] = emb
    gain = jnp.concatenate(
        [ln_single_s[i : i + 1, :] for i in range(ln_single_s.shape[0])], 1
    )
    y = layer_norm(emb, gain)
    y_ref[...] = y.astype(BF16)
    y_s[...] = y.reshape(y_s.shape)
    y_own = y_s[col].astype(BF16)
    hidden = w_out_s.shape[0]
    w_dist2 = doubled(w_dist_s[...])
    for b in range(blocks):
        z = pair_s[b * tile : (b + 1) * tile, :]
        xt = layer_norm(z, ln_trans_s[...]).astype(BF16)
        gu = jnp.dot(xt, w_in_s[...], preferred_element_type=F32)
        gate, up = gu[:, :hidden], gu[:, hidden:]
        hid = (gate * sigmoid(gate) * up).astype(BF16)
        new = z + jnp.dot(hid, w_out_s[...], preferred_element_type=F32)
        next_ref[b * tile : (b + 1) * tile, :] = new
        low = new.astype(BF16)
        pairs = [
            jnp.concatenate(
                [low[t * keys : (t + 1) * keys], low[(t + 1) * keys : (t + 2) * keys]], 1
            )
            for t in range(0, length, 2)
        ]
        proj = lax.dot_general(jnp.concatenate(pairs, 0), w_dist2, NT, preferred_element_type=F32)
        proj_s[b] = proj.reshape(length // 2, groups, length, lanes)
    for k in range(n_rows):
        to = row ^ k
        for b in range(blocks):
            for t in range(length // 2):
                out_refs[k][b, :, t * lanes : (t + 1) * lanes] = proj_s[b, t, to].astype(BF16)
        out_refs[k][blocks, :, :width] = y_own
        out_refs[k][blocks, :, width:] = jnp.zeros(
            (length, out_refs[k].shape[2] - width), BF16
        )


def bias_kernel(
    next_ref, ln_bias_ref, w_bias_ref, y_ref, w_attn_hbm, mask_ref,
    bias_ref, q_ref, keep_ref, w_kv_ref, w_q_s, sems,
):
    width = y_ref.shape[1]
    moves = [
        pltpu.make_async_copy(w_attn_hbm.at[:, pl.ds(0, width)], w_q_s, sems.at[0]),
        pltpu.make_async_copy(w_attn_hbm.at[:, pl.ds(width, 2 * width)], w_kv_ref, sems.at[1]),
    ]
    for move in moves:
        move.start()
    heads, channels = w_bias_ref.shape
    blocks, _, groups = mask_ref.shape
    queries = y_ref.shape[0]
    length = queries // blocks
    keys = groups * length
    lanes = length * heads
    tiled = jnp.concatenate([w_bias_ref[...]] * length, 0)
    owner = lax.broadcasted_iota(jnp.int32, tiled.shape, 0) // heads
    w_big = jnp.concatenate(
        [jnp.where(owner == t, tiled, jnp.zeros_like(tiled)) for t in range(length)], 1
    )
    rows = []
    for b in range(blocks):
        new = next_ref[b * length * keys : (b + 1) * length * keys, :]
        xb = layer_norm(new, ln_bias_ref[...]).astype(BF16)
        rows.append(
            jnp.concatenate([xb[t * keys : (t + 1) * keys] for t in range(length)], 1)
        )
    bias = lax.dot_general(jnp.concatenate(rows, 0), w_big, NT, preferred_element_type=F32)
    for b in range(blocks):
        bias_ref[:, b * lanes : (b + 1) * lanes] = bias[b * keys : (b + 1) * keys]
    for a in range(groups):
        for b in range(blocks):
            keep_ref[a * length : (a + 1) * length, b * lanes : (b + 1) * lanes] = (
                jnp.broadcast_to(mask_ref[b, :, a : a + 1], (length, lanes))
            )
    moves[0].wait()
    q = jnp.dot(y_ref[...], w_q_s[...], preferred_element_type=F32)
    q_ref[...] = (q * (width // heads) ** (-0.5)).astype(BF16)
    moves[1].wait()


def own_kernel(
    next_ref, w_dist_ref, dist_bias_ref, y_ref, w_attn_hbm, _,
    own_ref, gate_ref, next_hbm, w_gate_s, sems,
):
    width = y_ref.shape[1]
    moves = [
        pltpu.make_async_copy(w_attn_hbm.at[:, pl.ds(3 * width, width)], w_gate_s, sems.at[0]),
        pltpu.make_async_copy(next_ref, next_hbm, sems.at[1]),
    ]
    for move in moves:
        move.start()
    groups, blocks, length, wide = own_ref.shape
    keys, queries = groups * length, blocks * length
    bins = w_dist_ref.shape[0]
    w_dist2 = doubled(w_dist_ref[...])
    both = jnp.concatenate([dist_bias_ref[...]] * 2, 1)
    for a in range(groups):
        picked = []
        for t in range(0, length, 2):
            halves = [
                next_ref[pl.ds(a * length + t + s, queries, stride=keys), :].astype(BF16)
                for s in range(2)
            ]
            picked.append(jnp.concatenate(halves, 1))
        proj = lax.dot_general(jnp.concatenate(picked, 0), w_dist2, NT, preferred_element_type=F32)
        proj = proj.astype(BF16).astype(F32) + both
        for t in range(length // 2):
            own_ref[a, :, :, t * 2 * bins : (t + 1) * 2 * bins] = proj[
                t * queries : (t + 1) * queries
            ].reshape(blocks, length, 2 * bins)
    moves[0].wait()
    gate_ref[...] = sigmoid(jnp.dot(y_ref[...], w_gate_s[...], preferred_element_type=F32))
    moves[1].wait()


def attention_kernel(n_rows, n_cols, heads, q_ref, bias_ref, keep_ref, w_kv_ref, *rest):
    got_refs, out_refs, y_s = rest[:n_rows][::-1], rest[n_rows:-1], rest[-1]
    row, col = lax.axis_index("rows"), lax.axis_index("cols")
    groups, length, width = y_s.shape
    queries = q_ref.shape[0]
    blocks = queries // length
    keys = groups * length
    for k in range(n_rows):
        y_s[row ^ k] = got_refs[k][blocks, :, :width].astype(F32)
    y = y_s[...].reshape(keys, width).astype(BF16)
    kv = jnp.dot(y, w_kv_ref[...], preferred_element_type=F32).astype(BF16)
    mine = head_mask(heads, width)
    spread = jnp.where(mine[None], q_ref[...].astype(F32)[:, None, :], 0.0)
    spread = spread.reshape(queries * heads, width).astype(BF16)
    scores = lax.dot_general(kv[:, :width], spread, NT, preferred_element_type=F32)
    scores = jnp.where(keep_ref[...] > 0, scores + bias_ref[...], MASKED)
    top = jnp.max(scores, axis=0, keepdims=True)
    expo = jnp.exp(scores - top)
    total = jnp.sum(expo, axis=0, keepdims=True)
    acc = lax.dot_general(expo.astype(BF16), kv[:, width:], TN, preferred_element_type=F32)
    acc = jnp.sum(
        jnp.where(mine[None], acc.reshape(queries, heads, width), 0.0), axis=1
    )
    t0 = top.astype(BF16)
    t1 = (top - t0.astype(F32)).astype(BF16)
    t2 = (top - t0.astype(F32) - t1.astype(F32)).astype(BF16)
    s0 = total.astype(BF16)
    s1 = (total - s0.astype(F32)).astype(BF16)
    stats = jnp.concatenate([v.astype(F32) for v in (t0, t1, t2, s0, s1)], 0)
    stats = jnp.concatenate([stats, jnp.zeros((3, stats.shape[1]), F32)], 0).astype(BF16)
    room = out_refs[0].shape[2] - width
    piece = lax.broadcasted_iota(jnp.int32, (8, room), 0)
    lane = lax.broadcasted_iota(jnp.int32, (8, room), 1)
    place = (lane // heads == piece).astype(BF16)
    stats = lax.dot_general(stats, place, TN, preferred_element_type=F32)
    head = lax.broadcasted_iota(jnp.int32, (heads, room), 0)
    lane = lax.broadcasted_iota(jnp.int32, (heads, room), 1)
    stats = jnp.sum(
        jnp.where((lane % heads == head)[None], stats.reshape(queries, heads, room), 0.0), axis=1
    )
    part = jnp.concatenate([acc, stats], 1).reshape(blocks, length, width + room).astype(BF16)
    for k in range(n_cols):
        to = col ^ k
        for j in range(n_rows):
            out_refs[k][j] = got_refs[j][to]
        out_refs[k][n_rows:] = part


def tree_sum(values):
    while len(values) > 1:
        values = [values[i] + values[i + 1] for i in range(0, len(values), 2)]
    return values[0]


def final_kernel(
    n_rows, n_cols, order, heads, own_ref, emb_ref, gate_ref, w_out_ref, *rest
):
    got_refs = [rest[order.index(k)] for k in range(n_cols)]
    singles_hbm, logits_hbm, singles_ref, logits_ref, sems = rest[n_cols:]
    row, col = lax.axis_index("rows"), lax.axis_index("cols")
    groups, blocks, length, wide = own_ref.shape
    queries, width = emb_ref.shape
    for k in range(n_cols):
        source = col ^ k
        for a in range(groups):
            logits_ref[pl.ds(source * length, length), a, :] = (
                own_ref[a, source] + got_refs[k][row ^ a].astype(F32)
            )
    send_logits = pltpu.make_async_copy(logits_ref, logits_hbm, sems.at[0])
    send_logits.start()
    tops, sums, accs = [], [], []
    for k in range(n_cols):
        part = got_refs[k][n_rows:].astype(F32).reshape(queries, wide)
        accs.append(part[:, :width])
        piece = [part[:, width + heads * p : width + heads * (p + 1)] for p in range(5)]
        tops.append(piece[0] + piece[1] + piece[2])
        sums.append(piece[3] + piece[4])
    top = functools.reduce(jnp.maximum, tops)
    scale = [jnp.exp(t - top) for t in tops]
    total = tree_sum([s * w for s, w in zip(sums, scale)])
    share = jnp.concatenate([w / total for w in scale], 0)
    share = jnp.dot(
        share,
        head_mask(heads, width).astype(F32),
        precision=lax.Precision.HIGHEST,
        preferred_element_type=F32,
    )
    mixed = tree_sum([
        acc * share[k * queries : (k + 1) * queries] for k, acc in enumerate(accs)
    ])
    att = (gate_ref[...] * mixed).astype(BF16)
    singles_ref[...] = emb_ref[...] + jnp.dot(att, w_out_ref[...], preferred_element_type=F32)
    send_singles = pltpu.make_async_copy(singles_ref, singles_hbm, sems.at[1])
    send_singles.start()
    send_logits.wait()
    send_singles.wait()


def call(kernel, name, outs, scratch, flops, limit, *args, hbm_in=(), hbm_out=()):
    shapes = [jax.ShapeDtypeStruct(s, d) for s, d in outs]
    touched = sum(a.size * a.dtype.itemsize for a in (*args, *shapes))
    near = pl.BlockSpec(memory_space=pltpu.VMEM)
    far = pl.BlockSpec(memory_space=pltpu.HBM)
    return pl.pallas_call(
        kernel,
        name=name,
        out_shape=shapes,
        in_specs=[far if i in hbm_in else near for i in range(len(args))],
        out_specs=[far if i in hbm_out else near for i in range(len(shapes))],
        scratch_shapes=scratch,
        cost_estimate=pl.CostEstimate(flops=flops, bytes_accessed=touched, transcendentals=0),
        compiler_params=pltpu.CompilerParams(vmem_limit_bytes=limit),
    )(*args)


def local(
    n_rows, n_cols,
    pair, singles, restype, block_mask, ln_trans, w_trans_in, w_trans_out, ln_bias, w_bias,
    restype_table, ln_single, w_attn, w_single_out, w_dist, dist_bias,
):
    queries, groups, length, channels = pair.shape
    keys = groups * length
    blocks = queries // length
    heads = w_bias.shape[1]
    width = w_single_out.shape[0]
    bins = w_dist.shape[1]
    hidden = w_trans_out.shape[0]
    wide = length * bins
    rows = queries * keys
    mib = 1 << 20
    room = (16 if rows <= 2048 else 40) * mib
    inputs = [pltpu.with_memory_space_constraint(a, pltpu.HBM) for a in (
        pair.reshape(rows, channels), ln_trans[None], w_trans_in, w_trans_out, w_dist.T,
        singles, restype[None], restype_table, ln_single.reshape(-1, 128),
    )]
    first = call(
        functools.partial(transition_kernel, n_rows),
        "transition",
        [((rows, channels), F32), ((queries, width), F32), ((queries, width), BF16)]
        + [((blocks + 1, length, wide), BF16)] * n_rows,
        [
            pltpu.VMEM((blocks, length // 2, groups, length, 2 * bins), F32),
            pltpu.VMEM((blocks, length, width), F32),
            *[pltpu.VMEM(a.shape, a.dtype) for a in inputs],
            pltpu.SemaphoreType.DMA((len(inputs),)),
        ],
        2 * rows * channels * hidden * 3,
        room,
        *inputs,
        hbm_in=range(len(inputs)),
    )
    pair_next, emb, y, *blocks_out = first
    got = [blocks_out[0]] + [
        lax.ppermute(blocks_out[k], "rows", [(i, i ^ k) for i in range(n_rows)])
        for k in range(1, n_rows)
    ]
    w_attn_far = pltpu.with_memory_space_constraint(w_attn, pltpu.HBM)
    bias, q, keep, w_kv = call(
        bias_kernel,
        "bias",
        [
            ((keys, queries * heads), F32),
            ((queries, width), BF16),
            ((keys, queries * heads), jnp.int32),
            ((width, 2 * width), BF16),
        ],
        [pltpu.VMEM((width, width), BF16), pltpu.SemaphoreType.DMA((2,))],
        2 * rows * channels * 1024,
        room,
        pair_next, ln_bias[None], w_bias.T, y, w_attn_far, jnp.transpose(block_mask, (0, 2, 1)),
        hbm_in=(4,),
    )
    parts = call(
        functools.partial(attention_kernel, n_rows, n_cols, heads),
        "attention",
        [((groups + blocks, length, wide), BF16)] * n_cols,
        [pltpu.VMEM((groups, length, width), F32)],
        2 * rows * channels * 256,
        room,
        q, bias, keep, w_kv, *got[::-1],
    )
    mixed = [parts[0]] + [
        lax.ppermute(parts[k], "cols", [(i, i ^ k) for i in range(n_cols)])
        for k in range(1, n_cols)
    ]
    order = [k for k in range(1, n_cols) if k & (n_cols // 2)]
    order += [k for k in reversed(range(n_cols)) if k not in order]
    own, gate, pair_out = call(
        own_kernel,
        "own",
        [
            ((groups, blocks, length, wide), F32),
            ((queries, width), F32),
            ((rows, channels), F32),
        ],
        [pltpu.VMEM((width, width), BF16), pltpu.SemaphoreType.DMA((2,))],
        2 * rows * channels * 1024,
        room,
        pair_next, w_dist.T, dist_bias[None], y, w_attn_far, parts[0],
        hbm_in=(4,),
        hbm_out=(2,),
    )
    singles_next, dist_logits = call(
        functools.partial(final_kernel, n_rows, n_cols, order, heads),
        "final",
        [((queries, width), F32), ((queries, groups, wide), F32)],
        [
            pltpu.VMEM((queries, width), F32),
            pltpu.VMEM((queries, groups, wide), F32),
            pltpu.SemaphoreType.DMA((2,)),
        ],
        2 * rows * channels * 128,
        room,
        own, emb, gate, w_single_out, *[mixed[k] for k in order],
        hbm_out=(0, 1),
    )
    return pair_out.reshape(pair.shape), singles_next, dist_logits


def solution(mesh):
    return jax.shard_map(
        functools.partial(local, mesh.shape["rows"], mesh.shape["cols"]),
        mesh=mesh,
        in_specs=(
            P(("parts", "rows"), None, "cols", None),
            P(("parts", "rows"), None),
            P(("parts", "rows")),
            P(("parts", "rows"), None, "cols"),
            *([P()] * 11),
        ),
        out_specs=(
            P(("parts", "rows"), None, "cols", None),
            P(("parts", "rows"), None),
            P(("parts", "rows"), None, "cols"),
        ),
        check_vma=False,
    )
```

```python
import functools

import jax
import jax.numpy as jnp
from jax import lax
from jax.experimental import pallas as pl
from jax.experimental.pallas import tpu as pltpu
from jax.sharding import PartitionSpec as P

EPS = 1e-05
MASKED = -1000000000.0
HIDDEN = -1e30
F32, BF16 = jnp.float32, jnp.bfloat16
NT = (((1,), (1,)), ((), ()))
TN = (((0,), (0,)), ((), ()))


def layer_norm(values, gain_vec):
    average = jnp.mean(values, axis=-1, keepdims=True)
    centred = values - average
    spread = jnp.mean(centred * centred, axis=-1, keepdims=True)
    return centred * lax.rsqrt(spread + EPS) * gain_vec


def sigmoid(values):
    return 0.5 + 0.5 * jnp.tanh(0.5 * values)


def head_mask(heads, width):
    size = width // heads
    first = lax.broadcasted_iota(jnp.int32, (heads, width), 0) * size
    column = lax.broadcasted_iota(jnp.int32, (heads, width), 1)
    return jnp.logical_and(column >= first, column < first + size)


def doubled(w_t):
    zero = jnp.zeros_like(w_t)
    return jnp.concatenate(
        [jnp.concatenate([w_t, zero], 1), jnp.concatenate([zero, w_t], 1)], 0
    )


def y_places(blocks, width, lanes, across):
    pieces = [(b, at) for b in range(blocks) for at in range(0, width, lanes)]
    return [(b, at, i // across, i % across * lanes) for i, (b, at) in enumerate(pieces)]


def transition_kernel(
    n_rows,
    pair_hbm, ln_trans_hbm, w_in_hbm, w_out_hbm, w_dist_hbm,
    singles_hbm, restype_hbm, table_hbm, ln_single_hbm,
    next_ref, emb_ref, y_ref, *rest,
):
    out_refs, rest = rest[:n_rows], rest[n_rows:]
    (proj_s, pair_s, ln_trans_s, w_in_s, w_out_s, w_dist_s,
     singles_s, restype_s, table_s, ln_single_s, sems) = rest
    blocks, _, groups, length, lanes = proj_s.shape
    keys = groups * length
    tile = length * keys
    moves = [
        pltpu.make_async_copy(source, target, sems.at[i])
        for i, (source, target) in enumerate((
            (restype_hbm, restype_s), (table_hbm, table_s), (singles_hbm, singles_s),
            (ln_single_hbm, ln_single_s), (ln_trans_hbm, ln_trans_s), (w_in_hbm, w_in_s),
            (w_out_hbm, w_out_s), (w_dist_hbm, w_dist_s), (pair_hbm, pair_s),
        ))
    ]
    for move in moves:
        move.start()
    for move in moves:
        move.wait()
    row = lax.axis_index("rows")
    types = lax.broadcasted_iota(jnp.int32, (table_s.shape[0], restype_s.shape[1]), 0)
    one_hot = (types == restype_s[...]).astype(F32)
    emb = singles_s[...] + lax.dot_general(
        one_hot, table_s[...], TN, precision=lax.Precision.HIGHEST, preferred_element_type=F32
    )
    emb_ref[...] = emb
    gain = jnp.concatenate(
        [ln_single_s[i : i + 1, :] for i in range(ln_single_s.shape[0])], 1
    )
    y = layer_norm(emb, gain).astype(BF16)
    y_ref[...] = y
    hidden = w_out_s.shape[0]
    w_dist2 = doubled(w_dist_s[...])
    for b in range(blocks):
        z = pair_s[b * tile : (b + 1) * tile, :]
        xt = layer_norm(z, ln_trans_s[...]).astype(BF16)
        gu = jnp.dot(xt, w_in_s[...], preferred_element_type=F32)
        gate, up = gu[:, :hidden], gu[:, hidden:]
        hid = (gate * sigmoid(gate) * up).astype(BF16)
        new = z + jnp.dot(hid, w_out_s[...], preferred_element_type=F32)
        next_ref[b * tile : (b + 1) * tile, :] = new
        low = new.astype(BF16)
        pairs = [
            jnp.concatenate(
                [low[t * keys : (t + 1) * keys], low[(t + 1) * keys : (t + 2) * keys]], 1
            )
            for t in range(0, length, 2)
        ]
        proj = lax.dot_general(jnp.concatenate(pairs, 0), w_dist2, NT, preferred_element_type=F32)
        proj_s[b] = proj.reshape(length // 2, groups, length, lanes)
    for k in range(n_rows):
        to = row ^ k
        for b in range(blocks):
            for t in range(length // 2):
                out_refs[k][b, :, t * lanes : (t + 1) * lanes] = proj_s[b, t, to].astype(BF16)
        for b, across, group, at in y_places(blocks, y.shape[1], lanes, length // 2):
            out_refs[k][blocks + group, :, at : at + lanes] = y[
                b * length : (b + 1) * length, across : across + lanes
            ]


def bias_kernel(next_ref, ln_bias_ref, w_bias_ref, mask_ref, bias_ref):
    heads, channels = w_bias_ref.shape
    blocks, _, groups = mask_ref.shape
    keys, lanes = bias_ref.shape[0], bias_ref.shape[1] // blocks
    length = lanes // heads
    tiled = jnp.concatenate([w_bias_ref[...]] * length, 0)
    owner = lax.broadcasted_iota(jnp.int32, tiled.shape, 0) // heads
    w_big = jnp.concatenate(
        [jnp.where(owner == t, tiled, jnp.zeros_like(tiled)) for t in range(length)], 1
    )
    rows = []
    for b in range(blocks):
        new = next_ref[b * length * keys : (b + 1) * length * keys, :]
        xb = layer_norm(new, ln_bias_ref[...]).astype(BF16)
        rows.append(
            jnp.concatenate([xb[t * keys : (t + 1) * keys] for t in range(length)], 1)
        )
    bias = lax.dot_general(jnp.concatenate(rows, 0), w_big, NT, preferred_element_type=F32)
    for b in range(blocks):
        for a in range(groups):
            keep = jnp.broadcast_to(mask_ref[b, :, a : a + 1], (length, lanes)) > 0
            piece = bias[b * keys + a * length : b * keys + (a + 1) * length]
            bias_ref[a * length : (a + 1) * length, b * lanes : (b + 1) * lanes] = jnp.where(
                keep, piece, HIDDEN
            )


def repack_kernel(n_rows, n_cols, *refs):
    got_refs, out_refs = refs[:n_rows][::-1], refs[n_rows:]
    col = lax.axis_index("cols")
    for k in range(n_cols):
        to = col ^ k
        for j in range(n_rows):
            out_refs[k][j] = got_refs[j][to]


def own_kernel(
    next_ref, w_dist_ref, dist_bias_ref, w_attn_hbm, w_out_hbm, _,
    own_ref, w_attn_ref, w_out_ref, next_hbm, sems,
):
    moves = [
        pltpu.make_async_copy(w_attn_hbm, w_attn_ref, sems.at[0]),
        pltpu.make_async_copy(w_out_hbm, w_out_ref, sems.at[1]),
        pltpu.make_async_copy(next_ref, next_hbm, sems.at[2]),
    ]
    for move in moves:
        move.start()
    groups, blocks, length, wide = own_ref.shape
    keys, queries = groups * length, blocks * length
    bins = w_dist_ref.shape[0]
    w_dist2 = doubled(w_dist_ref[...])
    both = jnp.concatenate([dist_bias_ref[...]] * 2, 1)
    for a in range(groups):
        picked = []
        for t in range(0, length, 2):
            halves = [
                next_ref[pl.ds(a * length + t + s, queries, stride=keys), :].astype(BF16)
                for s in range(2)
            ]
            picked.append(jnp.concatenate(halves, 1))
        proj = lax.dot_general(jnp.concatenate(picked, 0), w_dist2, NT, preferred_element_type=F32)
        proj = proj.astype(BF16).astype(F32) + both
        for t in range(length // 2):
            own_ref[a, :, :, t * 2 * bins : (t + 1) * 2 * bins] = proj[
                t * queries : (t + 1) * queries
            ].reshape(blocks, length, 2 * bins)
    for move in moves:
        move.wait()


def attention_kernel(n_rows, n_cols, order, heads, y_ref, emb_ref, w_attn_ref, w_out_ref, *rest):
    got_refs, rest = rest[:n_rows][::-1], rest[n_rows:]
    bias_refs, (singles_ref, y_s, bias_s) = rest[:n_cols], rest[n_cols:]
    row, col = lax.axis_index("rows"), lax.axis_index("cols")
    blocks, groups, length, width = y_s.shape
    queries = y_ref.shape[0]
    keys = blocks * groups * length
    wide = got_refs[0].shape[2]
    for k in range(n_rows):
        for b, across, group, at in y_places(blocks, width, 128, wide // 128):
            y_s[b, row ^ k, :, across : across + 128] = got_refs[k][
                blocks + group, :, at : at + 128
            ].astype(F32)
    for k in range(n_cols):
        bias_s[col ^ k] = bias_refs[order.index(k)][...]
    y = y_s[...].reshape(keys, width).astype(BF16)
    kv = jnp.dot(y, w_attn_ref[:, width : 3 * width], preferred_element_type=F32).astype(BF16)
    q = jnp.dot(y_ref[...], w_attn_ref[:, :width], preferred_element_type=F32)
    q = (q * (width // heads) ** (-0.5)).astype(BF16)
    gate = sigmoid(jnp.dot(y_ref[...], w_attn_ref[:, 3 * width :], preferred_element_type=F32))
    mine = head_mask(heads, width)
    spread = jnp.where(mine[None], q.astype(F32)[:, None, :], 0.0)
    spread = spread.reshape(queries * heads, width).astype(BF16)
    scores = lax.dot_general(kv[:, :width], spread, NT, preferred_element_type=F32)
    bias = bias_s[...].reshape(keys, queries * heads)
    scores = jnp.where(bias > 0.5 * HIDDEN, scores + bias, MASKED)
    expo = jnp.exp(scores - jnp.max(scores, axis=0, keepdims=True))
    total = jnp.sum(expo, axis=0, keepdims=True)
    acc = lax.dot_general(expo.astype(BF16), kv[:, width:], TN, preferred_element_type=F32)
    total = jnp.transpose(jnp.broadcast_to(total, (8, queries * heads)))[:, :1]
    acc = (acc / total).reshape(queries, heads, width)
    mixed = jnp.sum(jnp.where(mine[None], acc, 0.0), axis=1)
    att = (gate * mixed).astype(BF16)
    singles_ref[...] = emb_ref[...] + jnp.dot(att, w_out_ref[...], preferred_element_type=F32)


def final_kernel(n_rows, n_cols, order, own_ref, *rest):
    got_refs = [rest[order.index(k)] for k in range(n_cols)]
    logits_ref = rest[n_cols]
    row, col = lax.axis_index("rows"), lax.axis_index("cols")
    groups, blocks, length, wide = own_ref.shape
    for k in range(n_cols):
        source = col ^ k
        for a in range(groups):
            logits_ref[pl.ds(source * length, length), a, :] = (
                own_ref[a, source] + got_refs[k][row ^ a].astype(F32)
            )


def call(kernel, name, outs, scratch, flops, limit, *args, hbm_in=(), hbm_out=()):
    shapes = [jax.ShapeDtypeStruct(s, d) for s, d in outs]
    touched = sum(a.size * a.dtype.itemsize for a in (*args, *shapes))
    near = pl.BlockSpec(memory_space=pltpu.VMEM)
    far = pl.BlockSpec(memory_space=pltpu.HBM)
    return pl.pallas_call(
        kernel,
        name=name,
        out_shape=shapes,
        in_specs=[far if i in hbm_in else near for i in range(len(args))],
        out_specs=[far if i in hbm_out else near for i in range(len(shapes))],
        scratch_shapes=scratch,
        cost_estimate=pl.CostEstimate(flops=flops, bytes_accessed=touched, transcendentals=0),
        compiler_params=pltpu.CompilerParams(vmem_limit_bytes=limit),
    )(*args)


def exchange(values, axis):
    size = len(values)
    return [values[0]] + [
        lax.ppermute(values[k], axis, [(i, i ^ k) for i in range(size)]) for k in range(1, size)
    ]


def local(
    n_rows, n_cols,
    pair, singles, restype, block_mask, ln_trans, w_trans_in, w_trans_out, ln_bias, w_bias,
    restype_table, ln_single, w_attn, w_single_out, w_dist, dist_bias,
):
    queries, groups, length, channels = pair.shape
    keys = groups * length
    blocks = queries // length
    heads = w_bias.shape[1]
    width = w_single_out.shape[0]
    bins = w_dist.shape[1]
    hidden = w_trans_out.shape[0]
    wide = length * bins
    rows = queries * keys
    mib = 1 << 20
    room = (16 if rows <= 2048 else 40) * mib
    inputs = [pltpu.with_memory_space_constraint(a, pltpu.HBM) for a in (
        pair.reshape(rows, channels), ln_trans[None], w_trans_in, w_trans_out, w_dist.T,
        singles, restype[None], restype_table, ln_single.reshape(-1, 128),
    )]
    y_groups = -(-blocks * (width // (2 * bins)) // (length // 2))
    first = call(
        functools.partial(transition_kernel, n_rows),
        "transition",
        [((rows, channels), F32), ((queries, width), F32), ((queries, width), BF16)]
        + [((blocks + y_groups, length, wide), BF16)] * n_rows,
        [
            pltpu.VMEM((blocks, length // 2, groups, length, 2 * bins), F32),
            *[pltpu.VMEM(a.shape, a.dtype) for a in inputs],
            pltpu.SemaphoreType.DMA((len(inputs),)),
        ],
        2 * rows * channels * hidden * 3,
        room,
        *inputs,
        hbm_in=range(len(inputs)),
    )
    pair_next, emb, y, *blocks_out = first
    got = exchange(blocks_out, "rows")
    (bias,) = call(
        bias_kernel,
        "bias",
        [((keys, queries * heads), F32)],
        [],
        2 * rows * channels * 1024,
        room,
        pair_next, ln_bias[None], w_bias.T, jnp.transpose(block_mask, (0, 2, 1)),
    )
    order = [k for k in range(1, n_cols) if k & (n_cols // 2)]
    order += [k for k in reversed(range(n_cols)) if k not in order]
    order_m = list(range(n_cols))[::-1]
    biases = exchange([bias] * n_cols, "cols")
    outgoing = call(
        functools.partial(repack_kernel, n_rows, n_cols),
        "repack",
        [((groups, length, wide), BF16)] * n_cols,
        [],
        2 * rows * channels * 64,
        room,
        *got[::-1],
    )
    mirrored = exchange(outgoing, "cols")
    far = [pltpu.with_memory_space_constraint(w, pltpu.HBM) for w in (w_attn, w_single_out)]
    own, w_attn_near, w_out_near, pair_out = call(
        own_kernel,
        "own",
        [
            ((groups, blocks, length, wide), F32),
            (w_attn.shape, BF16),
            (w_single_out.shape, BF16),
            ((rows, channels), F32),
        ],
        [pltpu.SemaphoreType.DMA((3,))],
        2 * rows * channels * 1024,
        room,
        pair_next, w_dist.T, dist_bias[None], *far, outgoing[0],
        hbm_in=(3, 4),
        hbm_out=(3,),
    )
    (singles_next,) = call(
        functools.partial(attention_kernel, n_rows, n_cols, order, heads),
        "attention",
        [((queries, width), F32)],
        [
            pltpu.VMEM((blocks, groups, length, width), F32),
            pltpu.VMEM((n_cols, keys, queries * heads), F32),
        ],
        2 * rows * channels * 1024,
        room,
        y, emb, w_attn_near, w_out_near, *got[::-1], *[biases[k] for k in order],
    )
    (dist_logits,) = call(
        functools.partial(final_kernel, n_rows, n_cols, order_m),
        "final",
        [((queries, groups, wide), F32)],
        [],
        2 * rows * channels * 128,
        room,
        own, *[mirrored[k] for k in order_m],
    )
    return pair_out.reshape(pair.shape), singles_next, dist_logits


def solution(mesh):
    return jax.shard_map(
        functools.partial(local, mesh.shape["rows"], mesh.shape["cols"]),
        mesh=mesh,
        in_specs=(
            P(("parts", "rows"), None, "cols", None),
            P(("parts", "rows"), None),
            P(("parts", "rows")),
            P(("parts", "rows"), None, "cols"),
            *([P()] * 11),
        ),
        out_specs=(
            P(("parts", "rows"), None, "cols", None),
            P(("parts", "rows"), None),
            P(("parts", "rows"), None, "cols"),
        ),
        check_vma=False,
    )
```

```python
import functools
import math

import jax
import jax.numpy as jnp
from jax import lax
from jax.experimental import pallas as pl
from jax.experimental.pallas import tpu as pltpu
from jax.sharding import PartitionSpec as P

EPS = 1e-05
MASKED = -1000000000.0
HIDDEN = -32768.0
F32, BF16 = jnp.float32, jnp.bfloat16
NT = (((1,), (1,)), ((), ()))
TN = (((0,), (0,)), ((), ()))


def layer_norm(values, gain_vec):
    average = jnp.mean(values, axis=-1, keepdims=True)
    centred = values - average
    spread = jnp.mean(centred * centred, axis=-1, keepdims=True)
    return centred * lax.rsqrt(spread + EPS) * gain_vec


def sigmoid(values):
    return 0.5 + 0.5 * jnp.tanh(0.5 * values)


def head_mask(heads, width):
    size = width // heads
    first = lax.broadcasted_iota(jnp.int32, (heads, width), 0) * size
    column = lax.broadcasted_iota(jnp.int32, (heads, width), 1)
    return jnp.logical_and(column >= first, column < first + size)


def bias_scale(channels):
    return 2.0 ** math.floor(math.log2(32767 / (0.96 * channels)))


def doubled(w_t):
    zero = jnp.zeros_like(w_t)
    return jnp.concatenate(
        [jnp.concatenate([w_t, zero], 1), jnp.concatenate([zero, w_t], 1)], 0
    )


def y_places(blocks, width, lanes, across):
    pieces = [(b, at) for b in range(blocks) for at in range(0, width, lanes)]
    return [(b, at, i // across, i % across * lanes) for i, (b, at) in enumerate(pieces)]


def queries_of(ref):
    return ref.shape[0] * ref.shape[1] * 2


def transition_kernel(
    n_rows,
    pair_hbm, ln_trans_hbm, w_in_hbm, w_out_hbm, w_dist_hbm,
    singles_hbm, restype_hbm, table_hbm, ln_single_hbm, w_attn_hbm, w_single_hbm,
    next_ref, emb_ref, y_ref, w_attn_ref, w_single_ref, *rest,
):
    out_refs, rest = rest[:n_rows], rest[n_rows:]
    (proj_s, pair_s, ln_trans_s, w_in_s, w_out_s, w_dist_s,
     singles_s, restype_s, table_s, ln_single_s, sems) = rest
    blocks, _, groups, length, lanes = proj_s.shape
    keys = groups * length
    tile = length * keys
    moves = [
        pltpu.make_async_copy(source, target, sems.at[i])
        for i, (source, target) in enumerate((
            (restype_hbm, restype_s), (table_hbm, table_s), (singles_hbm, singles_s),
            (ln_single_hbm, ln_single_s), (ln_trans_hbm, ln_trans_s), (pair_hbm, pair_s),
            (w_in_hbm, w_in_s), (w_out_hbm, w_out_s), (w_dist_hbm, w_dist_s),
        ))
    ]
    for move in moves:
        move.start()
    for move in moves[:4]:
        move.wait()
    row = lax.axis_index("rows")
    types = lax.broadcasted_iota(jnp.int32, (table_s.shape[0], restype_s.shape[1]), 0)
    one_hot = (types == restype_s[...]).astype(F32)
    emb = singles_s[...] + lax.dot_general(
        one_hot, table_s[...], TN, precision=lax.Precision.HIGHEST, preferred_element_type=F32
    )
    emb_ref[...] = emb
    gain = jnp.concatenate(
        [ln_single_s[i : i + 1, :] for i in range(ln_single_s.shape[0])], 1
    )
    y = layer_norm(emb, gain).astype(BF16)
    y_ref[...] = y
    for move in moves[4:]:
        move.wait()
    later = [
        pltpu.make_async_copy(w_attn_hbm, w_attn_ref, sems.at[len(moves)]),
        pltpu.make_async_copy(w_single_hbm, w_single_ref, sems.at[len(moves) + 1]),
    ]
    for move in later:
        move.start()
    hidden = w_out_s.shape[0]
    w_dist2 = doubled(w_dist_s[...])
    span, chunk = 16, 512
    for b in range(queries_of(proj_s) // span):
        z = pair_s[b * span * keys : (b + 1) * span * keys, :]
        xt = layer_norm(z, ln_trans_s[...]).astype(BF16)
        new = z
        for f in range(0, hidden, chunk):
            gate = jnp.dot(xt, w_in_s[:, f : f + chunk], preferred_element_type=F32)
            up = jnp.dot(xt, w_in_s[:, hidden + f : hidden + f + chunk], preferred_element_type=F32)
            hid = (gate * sigmoid(gate) * up).astype(BF16)
            new = new + jnp.dot(hid, w_out_s[f : f + chunk, :], preferred_element_type=F32)
        next_ref[b * span * keys : (b + 1) * span * keys, :] = new
        low = new.astype(BF16)
        pairs = [
            jnp.concatenate(
                [low[t * keys : (t + 1) * keys], low[(t + 1) * keys : (t + 2) * keys]], 1
            )
            for t in range(0, span, 2)
        ]
        proj = lax.dot_general(jnp.concatenate(pairs, 0), w_dist2, NT, preferred_element_type=F32)
        proj = proj.reshape(span // 2, groups, length, lanes)
        for t in range(span // 2):
            at = b * (span // 2) + t
            proj_s[at // (length // 2), at % (length // 2)] = proj[t]
    for k in range(n_rows):
        to = row ^ k
        for b in range(blocks):
            for t in range(length // 2):
                out_refs[k][b, :, t * lanes : (t + 1) * lanes] = proj_s[b, t, to].astype(BF16)
        for b, across, group, at in y_places(blocks, y.shape[1], lanes, length // 2):
            out_refs[k][blocks + group, :, at : at + lanes] = y[
                b * length : (b + 1) * length, across : across + lanes
            ]
    for move in later:
        move.wait()


def bias_kernel(next_ref, ln_bias_ref, w_bias_ref, mask_ref, bias_ref):
    heads, channels = w_bias_ref.shape
    blocks, _, groups = mask_ref.shape
    keys, lanes = bias_ref.shape[0], bias_ref.shape[1] // blocks
    length = lanes // heads
    tiled = jnp.concatenate([w_bias_ref[...]] * length, 0)
    owner = lax.broadcasted_iota(jnp.int32, tiled.shape, 0) // heads
    w_big = jnp.concatenate(
        [jnp.where(owner == t, tiled, jnp.zeros_like(tiled)) for t in range(length)], 1
    )
    rows = []
    for b in range(blocks):
        new = next_ref[b * length * keys : (b + 1) * length * keys, :]
        xb = layer_norm(new, ln_bias_ref[...]).astype(BF16)
        rows.append(
            jnp.concatenate([xb[t * keys : (t + 1) * keys] for t in range(length)], 1)
        )
    bias = lax.dot_general(jnp.concatenate(rows, 0), w_big, NT, preferred_element_type=F32)
    for b in range(blocks):
        for a in range(groups):
            keep = jnp.broadcast_to(mask_ref[b, :, a : a + 1], (length, lanes)) > 0
            piece = bias[b * keys + a * length : b * keys + (a + 1) * length]
            coded = jnp.where(keep, jnp.round(piece * bias_scale(channels)), HIDDEN).astype(jnp.int32)
            bias_ref[a * length : (a + 1) * length, b * lanes : (b + 1) * lanes] = coded.astype(
                jnp.int16
            )


def repack_kernel(n_rows, n_cols, *refs):
    got_refs, out_refs = refs[:n_rows][::-1], refs[n_rows:]
    col = lax.axis_index("cols")
    for k in range(n_cols):
        to = pick(ring_step(n_cols, k), col)
        for j in range(n_rows):
            out_refs[k][j] = got_refs[j][to]


def own_kernel(next_ref, w_dist_ref, dist_bias_ref, _, own_ref):
    groups, blocks, length, wide = own_ref.shape
    keys, queries = groups * length, blocks * length
    bins = w_dist_ref.shape[0]
    w_dist2 = doubled(w_dist_ref[...])
    both = jnp.concatenate([dist_bias_ref[...]] * 2, 1)
    for a in range(groups):
        picked = []
        for t in range(0, length, 2):
            halves = [
                next_ref[pl.ds(a * length + t + s, queries, stride=keys), :].astype(BF16)
                for s in range(2)
            ]
            picked.append(jnp.concatenate(halves, 1))
        proj = lax.dot_general(jnp.concatenate(picked, 0), w_dist2, NT, preferred_element_type=F32)
        proj = proj.astype(BF16).astype(F32) + both
        for t in range(length // 2):
            own_ref[a, :, :, t * 2 * bins : (t + 1) * 2 * bins] = proj[
                t * queries : (t + 1) * queries
            ].reshape(blocks, length, 2 * bins)


def attention_kernel(
    n_rows, n_cols, order, heads, scale, next_ref, y_ref, emb_ref, w_attn_ref, w_out_ref, *rest
):
    got_refs, rest = rest[:n_rows][::-1], rest[n_rows:]
    bias_refs, (_, singles_ref, next_hbm, y_s, bias_s, sem) = rest[:n_cols], rest[n_cols:]
    move = pltpu.make_async_copy(next_ref, next_hbm, sem)
    move.start()
    row, col = lax.axis_index("rows"), lax.axis_index("cols")
    blocks, groups, length, width = y_s.shape
    queries = y_ref.shape[0]
    keys = blocks * groups * length
    wide = got_refs[0].shape[2]
    for k in range(n_rows):
        for b, across, group, at in y_places(blocks, width, 128, wide // 128):
            y_s[b, row ^ k, :, across : across + 128] = got_refs[k][
                blocks + group, :, at : at + 128
            ].astype(F32)
    for k in range(n_cols):
        bias_s[pick(ring_step(n_cols, n_cols - k), col)] = bias_refs[order.index(k)][...].astype(jnp.int32).astype(F32)
    y = y_s[...].reshape(keys, width).astype(BF16)
    kv = jnp.dot(y, w_attn_ref[:, width : 3 * width], preferred_element_type=F32).astype(BF16)
    q = jnp.dot(y_ref[...], w_attn_ref[:, :width], preferred_element_type=F32)
    q = (q * (width // heads) ** (-0.5)).astype(BF16)
    gate = sigmoid(jnp.dot(y_ref[...], w_attn_ref[:, 3 * width :], preferred_element_type=F32))
    mine = head_mask(heads, width)
    spread = jnp.where(mine[None], q.astype(F32)[:, None, :], 0.0)
    spread = spread.reshape(queries * heads, width).astype(BF16)
    scores = lax.dot_general(kv[:, :width], spread, NT, preferred_element_type=F32)
    bias = bias_s[...].reshape(keys, queries * heads)
    scores = jnp.where(bias > HIDDEN, scores + bias * (1.0 / scale), MASKED)
    expo = jnp.exp(scores - jnp.max(scores, axis=0, keepdims=True))
    total = jnp.sum(expo, axis=0, keepdims=True)
    acc = lax.dot_general(expo.astype(BF16), kv[:, width:], TN, preferred_element_type=F32)
    total = jnp.transpose(jnp.broadcast_to(total, (8, queries * heads)))[:, :1]
    acc = (acc / total).reshape(queries, heads, width)
    mixed = jnp.sum(jnp.where(mine[None], acc, 0.0), axis=1)
    att = (gate * mixed).astype(BF16)
    singles_ref[...] = emb_ref[...] + jnp.dot(att, w_out_ref[...], preferred_element_type=F32)
    move.wait()


def final_kernel(n_rows, n_cols, order, own_ref, singles_ref, *rest):
    got_refs = [rest[order.index(k)] for k in range(n_cols)]
    singles_hbm, logits_hbm, logits_s, sems = rest[n_cols:]
    moves = [
        pltpu.make_async_copy(singles_ref, singles_hbm, sems.at[0]),
        pltpu.make_async_copy(logits_s, logits_hbm, sems.at[1]),
    ]
    moves[0].start()
    row, col = lax.axis_index("rows"), lax.axis_index("cols")
    groups, blocks, length, wide = own_ref.shape
    for k in range(n_cols):
        source = pick(ring_step(n_cols, n_cols - k), col)
        for a in range(groups):
            logits_s[pl.ds(source * length, length), a, :] = (
                own_ref[a, source] + got_refs[k][row ^ a].astype(F32)
            )
    moves[1].start()
    for move in moves:
        move.wait()


def call(kernel, name, outs, scratch, flops, limit, *args, hbm_in=(), hbm_out=()):
    shapes = [jax.ShapeDtypeStruct(s, d) for s, d in outs]
    touched = sum(a.size * a.dtype.itemsize for a in (*args, *shapes))
    near = pl.BlockSpec(memory_space=pltpu.VMEM)
    far = pl.BlockSpec(memory_space=pltpu.HBM)
    return pl.pallas_call(
        kernel,
        name=name,
        out_shape=shapes,
        in_specs=[far if i in hbm_in else near for i in range(len(args))],
        out_specs=[far if i in hbm_out else near for i in range(len(shapes))],
        scratch_shapes=scratch,
        cost_estimate=pl.CostEstimate(flops=flops, bytes_accessed=touched, transcendentals=0),
        compiler_params=pltpu.CompilerParams(vmem_limit_bytes=limit),
    )(*args)


def ring_step(size, step):
    ring = [0, *range(1, size, 2), *reversed(range(2, size, 2))]
    return [ring[(ring.index(i) + step) % size] for i in range(size)]


def pick(table, index):
    return sum(jnp.where(index == i, v, 0) for i, v in enumerate(table))


def exchange_line(values, axis):
    size = len(values)
    return [values[0]] + [
        lax.ppermute(values[k], axis, list(enumerate(ring_step(size, k)))) for k in range(1, size)
    ]


def exchange(values, axis):
    size = len(values)
    return [values[0]] + [
        lax.ppermute(values[k], axis, [(i, i ^ k) for i in range(size)]) for k in range(1, size)
    ]


def local(
    n_rows, n_cols,
    pair, singles, restype, block_mask, ln_trans, w_trans_in, w_trans_out, ln_bias, w_bias,
    restype_table, ln_single, w_attn, w_single_out, w_dist, dist_bias,
):
    queries, groups, length, channels = pair.shape
    keys = groups * length
    blocks = queries // length
    heads = w_bias.shape[1]
    width = w_single_out.shape[0]
    bins = w_dist.shape[1]
    hidden = w_trans_out.shape[0]
    wide = length * bins
    rows = queries * keys
    mib = 1 << 20
    room = (16 if rows <= 2048 else 40) * mib
    inputs = [pltpu.with_memory_space_constraint(a, pltpu.HBM) for a in (
        pair.reshape(rows, channels), ln_trans[None], w_trans_in, w_trans_out, w_dist.T,
        singles, restype[None], restype_table, ln_single.reshape(-1, 128), w_attn, w_single_out,
    )]
    y_groups = -(-blocks * (width // (2 * bins)) // (length // 2))
    first = call(
        functools.partial(transition_kernel, n_rows),
        "transition",
        [
            ((rows, channels), F32),
            ((queries, width), F32),
            ((queries, width), BF16),
            (w_attn.shape, BF16),
            (w_single_out.shape, BF16),
        ]
        + [((blocks + y_groups, length, wide), BF16)] * n_rows,
        [
            pltpu.VMEM((blocks, length // 2, groups, length, 2 * bins), F32),
            *[pltpu.VMEM(a.shape, a.dtype) for a in inputs[:-2]],
            pltpu.SemaphoreType.DMA((len(inputs),)),
        ],
        2 * rows * channels * hidden * 3,
        room,
        *inputs,
        hbm_in=range(len(inputs)),
    )
    pair_next, emb, y, w_attn_near, w_single_near, *blocks_out = first
    got = exchange(blocks_out, "rows")
    (bias,) = call(
        bias_kernel,
        "bias",
        [((keys, queries * heads), jnp.int16)],
        [],
        2 * rows * channels * 1024,
        room,
        pair_next, ln_bias[None], w_bias.T, jnp.transpose(block_mask, (0, 2, 1)),
    )
    order = [n_cols // 2] + [k for k in range(1, n_cols) if k != n_cols // 2] + [0]
    order_m = [*range(1, n_cols), 0]
    biases = exchange_line([bias] * n_cols, "cols")
    outgoing = call(
        functools.partial(repack_kernel, n_rows, n_cols),
        "repack",
        [((groups, length, wide), BF16)] * n_cols,
        [],
        2 * rows * channels * 64,
        room,
        *got[::-1],
    )
    mirrored = exchange_line(outgoing, "cols")
    (own,) = call(
        own_kernel,
        "own",
        [((groups, blocks, length, wide), F32)],
        [],
        2 * rows * channels * 1024,
        room,
        pair_next, w_dist.T, dist_bias[None], outgoing[0],
    )
    singles_near, pair_out = call(
        functools.partial(attention_kernel, n_rows, n_cols, order, heads, bias_scale(channels)),
        "attention",
        [((queries, width), F32), ((rows, channels), F32)],
        [
            pltpu.VMEM((blocks, groups, length, width), F32),
            pltpu.VMEM((n_cols, keys, queries * heads), F32),
            pltpu.SemaphoreType.DMA,
        ],
        2 * rows * channels * 1024,
        room,
        pair_next, y, emb, w_attn_near, w_single_near,
        *got[::-1], *[biases[k] for k in order], own,
        hbm_out=(1,),
    )
    singles_next, dist_logits = call(
        functools.partial(final_kernel, n_rows, n_cols, order_m),
        "final",
        [((queries, width), F32), ((queries, groups, wide), F32)],
        [pltpu.VMEM((queries, groups, wide), F32), pltpu.SemaphoreType.DMA((2,))],
        2 * rows * channels * 128,
        room,
        own, singles_near, *[mirrored[k] for k in order_m],
        hbm_out=(0, 1),
    )
    return pair_out.reshape(pair.shape), singles_next, dist_logits


def solution(mesh):
    return jax.shard_map(
        functools.partial(local, mesh.shape["rows"], mesh.shape["cols"]),
        mesh=mesh,
        in_specs=(
            P(("parts", "rows"), None, "cols", None),
            P(("parts", "rows"), None),
            P(("parts", "rows")),
            P(("parts", "rows"), None, "cols"),
            *([P()] * 11),
        ),
        out_specs=(
            P(("parts", "rows"), None, "cols", None),
            P(("parts", "rows"), None),
            P(("parts", "rows"), None, "cols"),
        ),
        check_vma=False,
    )
```

```python
import functools
import math

import jax
import jax.numpy as jnp
from jax import lax
from jax.experimental import pallas as pl
from jax.experimental.pallas import tpu as pltpu
from jax.sharding import PartitionSpec as P

EPS = 1e-05
MASKED = -1000000000.0
HIDDEN = -32768.0
F32, BF16 = jnp.float32, jnp.bfloat16
NT = (((1,), (1,)), ((), ()))
TN = (((0,), (0,)), ((), ()))


def layer_norm(values, gain_vec):
    average = jnp.mean(values, axis=-1, keepdims=True)
    centred = values - average
    size = values.shape[-1]
    spread = jnp.sum(centred * centred, axis=-1, keepdims=True)
    return centred * lax.rsqrt(spread + size * EPS) * (gain_vec * math.sqrt(size))


def sigmoid(values):
    return 0.5 + 0.5 * jnp.tanh(0.5 * values)


def head_mask(heads, width):
    size = width // heads
    first = lax.broadcasted_iota(jnp.int32, (heads, width), 0) * size
    column = lax.broadcasted_iota(jnp.int32, (heads, width), 1)
    return jnp.logical_and(column >= first, column < first + size)


def bias_scale(channels):
    return 2.0 ** math.floor(math.log2(32767 / (0.96 * channels)))


def doubled(w_t):
    zero = jnp.zeros_like(w_t)
    return jnp.concatenate(
        [jnp.concatenate([w_t, zero], 1), jnp.concatenate([zero, w_t], 1)], 0
    )


def y_places(blocks, width, lanes, across):
    pieces = [(b, at) for b in range(blocks) for at in range(0, width, lanes)]
    return [(b, at, i // across, i % across * lanes) for i, (b, at) in enumerate(pieces)]


def queries_of(ref):
    return ref.shape[0] * ref.shape[1] * 2


def transition_kernel(
    n_rows,
    pair_hbm, ln_trans_hbm, w_in_hbm, w_out_hbm, w_dist_hbm,
    singles_hbm, restype_hbm, table_hbm, ln_single_hbm, w_attn_hbm, w_single_hbm,
    next_ref, emb_ref, y_ref, w_attn_ref, w_single_ref, *rest,
):
    out_refs, rest = rest[:n_rows], rest[n_rows:]
    (proj_s, pair_s, ln_trans_s, w_in_s, w_out_s, w_dist_s,
     singles_s, restype_s, table_s, ln_single_s, sems) = rest
    blocks, _, groups, length, lanes = proj_s.shape
    keys = groups * length
    tile = length * keys
    moves = [
        pltpu.make_async_copy(source, target, sems.at[i])
        for i, (source, target) in enumerate((
            (restype_hbm, restype_s), (table_hbm, table_s), (singles_hbm, singles_s),
            (ln_single_hbm, ln_single_s), (ln_trans_hbm, ln_trans_s), (pair_hbm, pair_s),
            (w_in_hbm, w_in_s), (w_out_hbm, w_out_s), (w_dist_hbm, w_dist_s),
        ))
    ]
    for move in moves:
        move.start()
    for move in moves[:4]:
        move.wait()
    row = lax.axis_index("rows")
    types = lax.broadcasted_iota(jnp.int32, (table_s.shape[0], restype_s.shape[1]), 0)
    one_hot = (types == restype_s[...]).astype(F32)
    emb = singles_s[...] + lax.dot_general(
        one_hot, table_s[...], TN, precision=lax.Precision.HIGHEST, preferred_element_type=F32
    )
    emb_ref[...] = emb
    gain = jnp.concatenate(
        [ln_single_s[i : i + 1, :] for i in range(ln_single_s.shape[0])], 1
    )
    y = layer_norm(emb, gain).astype(BF16)
    y_ref[...] = y
    for move in moves[4:]:
        move.wait()
    later = [
        pltpu.make_async_copy(w_attn_hbm, w_attn_ref, sems.at[len(moves)]),
        pltpu.make_async_copy(w_single_hbm, w_single_ref, sems.at[len(moves) + 1]),
    ]
    for move in later:
        move.start()
    hidden = w_out_s.shape[0]
    w_dist2 = doubled(w_dist_s[...])
    w_in_s[:, :hidden] = w_in_s[:, :hidden] * jnp.asarray(0.5, BF16)
    span = 4
    count = queries_of(proj_s) // span

    def open_tile(b):
        z = pair_s[b * span * keys : (b + 1) * span * keys, :]
        xt = layer_norm(z, ln_trans_s[...]).astype(BF16)
        return jnp.dot(xt, w_in_s[...], preferred_element_type=F32)

    def gated(gu):
        half, up = gu[:, :hidden], gu[:, hidden:]
        return ((half + half * jnp.tanh(half)) * up).astype(BF16)

    def close_tile(b, hid):
        at = slice(b * span * keys, (b + 1) * span * keys)
        new = pair_s[at, :] + jnp.dot(hid, w_out_s[...], preferred_element_type=F32)
        next_ref[at, :] = new
        return new.astype(BF16)

    def project(b, low):
        pairs = [
            jnp.concatenate(
                [low[t * keys : (t + 1) * keys], low[(t + 1) * keys : (t + 2) * keys]], 1
            )
            for t in range(0, span, 2)
        ]
        proj = lax.dot_general(jnp.concatenate(pairs, 0), w_dist2, NT, preferred_element_type=F32)
        proj = proj.reshape(span // 2, groups, length, lanes)
        for t in range(span // 2):
            at = b * (span // 2) + t
            proj_s[at // (length // 2), at % (length // 2)] = proj[t]

    gus, lows = {0: open_tile(0)}, {}
    for b in range(count):
        if b + 1 < count:
            gus[b + 1] = open_tile(b + 1)
        lows[b] = close_tile(b, gated(gus.pop(b)))
    for b in range(count):
        project(b, lows.pop(b))
    for k in range(n_rows):
        to = row ^ k
        for b in range(blocks):
            for t in range(length // 2):
                out_refs[k][b, :, t * lanes : (t + 1) * lanes] = proj_s[b, t, to].astype(BF16)
        for b, across, group, at in y_places(blocks, y.shape[1], lanes, length // 2):
            out_refs[k][blocks + group, :, at : at + lanes] = y[
                b * length : (b + 1) * length, across : across + lanes
            ]
    for move in later:
        move.wait()


def bias_kernel(next_ref, ln_bias_ref, w_bias_ref, mask_ref, bias_ref):
    heads, channels = w_bias_ref.shape
    blocks, _, groups = mask_ref.shape
    keys, lanes = bias_ref.shape[0], bias_ref.shape[1] // blocks
    length = lanes // heads
    tiled = jnp.concatenate([w_bias_ref[...]] * length, 0)
    owner = lax.broadcasted_iota(jnp.int32, tiled.shape, 0) // heads
    w_big = jnp.concatenate(
        [jnp.where(owner == t, tiled, jnp.zeros_like(tiled)) for t in range(length)], 1
    )
    rows = []
    for b in range(blocks):
        new = next_ref[b * length * keys : (b + 1) * length * keys, :]
        xb = layer_norm(new, ln_bias_ref[...]).astype(BF16)
        rows.append(
            jnp.concatenate([xb[t * keys : (t + 1) * keys] for t in range(length)], 1)
        )
    bias = lax.dot_general(jnp.concatenate(rows, 0), w_big, NT, preferred_element_type=F32)
    for b in range(blocks):
        for a in range(groups):
            keep = jnp.broadcast_to(mask_ref[b, :, a : a + 1], (length, lanes)) > 0
            piece = bias[b * keys + a * length : b * keys + (a + 1) * length]
            coded = jnp.where(keep, jnp.round(piece * bias_scale(channels)), HIDDEN).astype(jnp.int32)
            bias_ref[a * length : (a + 1) * length, b * lanes : (b + 1) * lanes] = coded.astype(
                jnp.int16
            )


def repack_kernel(n_rows, n_cols, *refs):
    got_refs, out_refs = refs[:n_rows][::-1], refs[n_rows:]
    col = lax.axis_index("cols")
    for k in range(n_cols):
        to = pick(ring_step(n_cols, k), col)
        for j in range(n_rows):
            out_refs[k][j] = got_refs[j][to]


def own_kernel(next_ref, w_dist_ref, dist_bias_ref, _, own_ref):
    groups, blocks, length, wide = own_ref.shape
    keys, queries = groups * length, blocks * length
    bins = w_dist_ref.shape[0]
    w_dist2 = doubled(w_dist_ref[...])
    both = jnp.concatenate([dist_bias_ref[...]] * 2, 1)
    for a in range(groups):
        picked = []
        for t in range(0, length, 2):
            halves = [
                next_ref[pl.ds(a * length + t + s, queries, stride=keys), :].astype(BF16)
                for s in range(2)
            ]
            picked.append(jnp.concatenate(halves, 1))
        proj = lax.dot_general(jnp.concatenate(picked, 0), w_dist2, NT, preferred_element_type=F32)
        proj = proj.astype(BF16).astype(F32) + both
        for t in range(length // 2):
            own_ref[a, :, :, t * 2 * bins : (t + 1) * 2 * bins] = proj[
                t * queries : (t + 1) * queries
            ].reshape(blocks, length, 2 * bins)


def attention_kernel(
    n_rows, n_cols, order, heads, scale, next_ref, y_ref, emb_ref, w_attn_ref, w_out_ref, *rest
):
    got_refs, rest = rest[:n_rows][::-1], rest[n_rows:]
    bias_refs, (_, singles_ref, next_hbm, y_s, bias_s, sem) = rest[:n_cols], rest[n_cols:]
    move = pltpu.make_async_copy(next_ref, next_hbm, sem)
    move.start()
    row, col = lax.axis_index("rows"), lax.axis_index("cols")
    blocks, groups, length, width = y_s.shape
    queries = y_ref.shape[0]
    keys = blocks * groups * length
    wide = got_refs[0].shape[2]
    for k in range(n_rows):
        for b, across, group, at in y_places(blocks, width, 128, wide // 128):
            y_s[b, row ^ k, :, across : across + 128] = got_refs[k][
                blocks + group, :, at : at + 128
            ].astype(F32)
    for k in range(n_cols):
        bias_s[pick(ring_step(n_cols, n_cols - k), col)] = bias_refs[order.index(k)][...].astype(jnp.int32).astype(F32)
    y = y_s[...].reshape(keys, width).astype(BF16)
    kv = jnp.dot(y, w_attn_ref[:, width : 3 * width], preferred_element_type=F32).astype(BF16)
    q = jnp.dot(y_ref[...], w_attn_ref[:, :width], preferred_element_type=F32)
    q = (q * (width // heads) ** (-0.5)).astype(BF16)
    gate = sigmoid(jnp.dot(y_ref[...], w_attn_ref[:, 3 * width :], preferred_element_type=F32))
    mine = head_mask(heads, width)
    spread = jnp.where(mine[None], q.astype(F32)[:, None, :], 0.0)
    spread = spread.reshape(queries * heads, width).astype(BF16)
    scores = lax.dot_general(kv[:, :width], spread, NT, preferred_element_type=F32)
    bias = bias_s[...].reshape(keys, queries * heads)
    scores = jnp.where(bias > HIDDEN, scores + bias * (1.0 / scale), MASKED)
    expo = jnp.exp(scores - jnp.max(scores, axis=0, keepdims=True))
    total = jnp.sum(expo, axis=0, keepdims=True)
    acc = lax.dot_general(expo.astype(BF16), kv[:, width:], TN, preferred_element_type=F32)
    total = jnp.transpose(jnp.broadcast_to(total, (8, queries * heads)))[:, :1]
    acc = (acc / total).reshape(queries, heads, width)
    mixed = jnp.sum(jnp.where(mine[None], acc, 0.0), axis=1)
    att = (gate * mixed).astype(BF16)
    singles_ref[...] = emb_ref[...] + jnp.dot(att, w_out_ref[...], preferred_element_type=F32)
    move.wait()


def final_kernel(n_rows, n_cols, order, own_ref, singles_ref, *rest):
    got_refs = [rest[order.index(k)] for k in range(n_cols)]
    singles_hbm, logits_hbm, logits_s, sems = rest[n_cols:]
    moves = [
        pltpu.make_async_copy(singles_ref, singles_hbm, sems.at[0]),
        pltpu.make_async_copy(logits_s, logits_hbm, sems.at[1]),
    ]
    moves[0].start()
    row, col = lax.axis_index("rows"), lax.axis_index("cols")
    groups, blocks, length, wide = own_ref.shape
    for k in range(n_cols):
        source = pick(ring_step(n_cols, n_cols - k), col)
        for a in range(groups):
            logits_s[pl.ds(source * length, length), a, :] = (
                own_ref[a, source] + got_refs[k][row ^ a].astype(F32)
            )
    moves[1].start()
    for move in moves:
        move.wait()


def call(kernel, name, outs, scratch, flops, limit, *args, hbm_in=(), hbm_out=()):
    shapes = [jax.ShapeDtypeStruct(s, d) for s, d in outs]
    touched = sum(a.size * a.dtype.itemsize for a in (*args, *shapes))
    near = pl.BlockSpec(memory_space=pltpu.VMEM)
    far = pl.BlockSpec(memory_space=pltpu.HBM)
    return pl.pallas_call(
        kernel,
        name=name,
        out_shape=shapes,
        in_specs=[far if i in hbm_in else near for i in range(len(args))],
        out_specs=[far if i in hbm_out else near for i in range(len(shapes))],
        scratch_shapes=scratch,
        cost_estimate=pl.CostEstimate(flops=flops, bytes_accessed=touched, transcendentals=0),
        compiler_params=pltpu.CompilerParams(vmem_limit_bytes=limit),
    )(*args)


def ring_step(size, step):
    ring = [0, *range(1, size, 2), *reversed(range(2, size, 2))]
    return [ring[(ring.index(i) + step) % size] for i in range(size)]


def pick(table, index):
    return sum(jnp.where(index == i, v, 0) for i, v in enumerate(table))


def exchange_line(values, axis):
    size = len(values)
    return [values[0]] + [
        lax.ppermute(values[k], axis, list(enumerate(ring_step(size, k)))) for k in range(1, size)
    ]


def exchange(values, axis):
    size = len(values)
    return [values[0]] + [
        lax.ppermute(values[k], axis, [(i, i ^ k) for i in range(size)]) for k in range(1, size)
    ]


def local(
    n_rows, n_cols,
    pair, singles, restype, block_mask, ln_trans, w_trans_in, w_trans_out, ln_bias, w_bias,
    restype_table, ln_single, w_attn, w_single_out, w_dist, dist_bias,
):
    queries, groups, length, channels = pair.shape
    keys = groups * length
    blocks = queries // length
    heads = w_bias.shape[1]
    width = w_single_out.shape[0]
    bins = w_dist.shape[1]
    hidden = w_trans_out.shape[0]
    wide = length * bins
    rows = queries * keys
    mib = 1 << 20
    room = (16 if rows <= 2048 else 40) * mib
    inputs = [pltpu.with_memory_space_constraint(a, pltpu.HBM) for a in (
        pair.reshape(rows, channels), ln_trans[None], w_trans_in, w_trans_out, w_dist.T,
        singles, restype[None], restype_table, ln_single.reshape(-1, 128), w_attn, w_single_out,
    )]
    y_groups = -(-blocks * (width // (2 * bins)) // (length // 2))
    first = call(
        functools.partial(transition_kernel, n_rows),
        "transition",
        [
            ((rows, channels), F32),
            ((queries, width), F32),
            ((queries, width), BF16),
            (w_attn.shape, BF16),
            (w_single_out.shape, BF16),
        ]
        + [((blocks + y_groups, length, wide), BF16)] * n_rows,
        [
            pltpu.VMEM((blocks, length // 2, groups, length, 2 * bins), F32),
            *[pltpu.VMEM(a.shape, a.dtype) for a in inputs[:-2]],
            pltpu.SemaphoreType.DMA((len(inputs),)),
        ],
        2 * rows * channels * hidden * 3,
        room,
        *inputs,
        hbm_in=range(len(inputs)),
    )
    pair_next, emb, y, w_attn_near, w_single_near, *blocks_out = first
    got = exchange(blocks_out, "rows")
    (bias,) = call(
        bias_kernel,
        "bias",
        [((keys, queries * heads), jnp.int16)],
        [],
        2 * rows * channels * 1024,
        room,
        pair_next, ln_bias[None], w_bias.T, jnp.transpose(block_mask, (0, 2, 1)),
    )
    order = [n_cols // 2] + [k for k in range(1, n_cols) if k != n_cols // 2] + [0]
    order_m = [*range(1, n_cols), 0]
    biases = exchange_line([bias] * n_cols, "cols")
    outgoing = call(
        functools.partial(repack_kernel, n_rows, n_cols),
        "repack",
        [((groups, length, wide), BF16)] * n_cols,
        [],
        2 * rows * channels * 64,
        room,
        *got[::-1],
    )
    mirrored = exchange_line(outgoing, "cols")
    (own,) = call(
        own_kernel,
        "own",
        [((groups, blocks, length, wide), F32)],
        [],
        2 * rows * channels * 1024,
        room,
        pair_next, w_dist.T, dist_bias[None], outgoing[0],
    )
    singles_near, pair_out = call(
        functools.partial(attention_kernel, n_rows, n_cols, order, heads, bias_scale(channels)),
        "attention",
        [((queries, width), F32), ((rows, channels), F32)],
        [
            pltpu.VMEM((blocks, groups, length, width), F32),
            pltpu.VMEM((n_cols, keys, queries * heads), F32),
            pltpu.SemaphoreType.DMA,
        ],
        2 * rows * channels * 1024,
        room,
        pair_next, y, emb, w_attn_near, w_single_near,
        *got[::-1], *[biases[k] for k in order], own,
        hbm_out=(1,),
    )
    singles_next, dist_logits = call(
        functools.partial(final_kernel, n_rows, n_cols, order_m),
        "final",
        [((queries, width), F32), ((queries, groups, wide), F32)],
        [pltpu.VMEM((queries, groups, wide), F32), pltpu.SemaphoreType.DMA((2,))],
        2 * rows * channels * 128,
        room,
        own, singles_near, *[mirrored[k] for k in order_m],
        hbm_out=(0, 1),
    )
    return pair_out.reshape(pair.shape), singles_next, dist_logits


def solution(mesh):
    return jax.shard_map(
        functools.partial(local, mesh.shape["rows"], mesh.shape["cols"]),
        mesh=mesh,
        in_specs=(
            P(("parts", "rows"), None, "cols", None),
            P(("parts", "rows"), None),
            P(("parts", "rows")),
            P(("parts", "rows"), None, "cols"),
            *([P()] * 11),
        ),
        out_specs=(
            P(("parts", "rows"), None, "cols", None),
            P(("parts", "rows"), None),
            P(("parts", "rows"), None, "cols"),
        ),
        check_vma=False,
    )
```

```python
import functools
import math

import jax
import jax.numpy as jnp
from jax import lax
from jax.experimental import pallas as pl
from jax.experimental.pallas import tpu as pltpu
from jax.sharding import PartitionSpec as P

EPS = 1e-05
MASKED = -1000000000.0
HIDDEN = -32768.0
F32, BF16 = jnp.float32, jnp.bfloat16
NT = (((1,), (1,)), ((), ()))
TN = (((0,), (0,)), ((), ()))


def layer_norm(values, gain_vec):
    average = jnp.mean(values, axis=-1, keepdims=True)
    centred = values - average
    size = values.shape[-1]
    spread = jnp.sum(centred * centred, axis=-1, keepdims=True)
    return centred * lax.rsqrt(spread + size * EPS) * (gain_vec * math.sqrt(size))


def sigmoid(values):
    return 0.5 + 0.5 * jnp.tanh(0.5 * values)


def head_mask(heads, width):
    size = width // heads
    first = lax.broadcasted_iota(jnp.int32, (heads, width), 0) * size
    column = lax.broadcasted_iota(jnp.int32, (heads, width), 1)
    return jnp.logical_and(column >= first, column < first + size)


def bias_scale(channels):
    return 2.0 ** math.floor(math.log2(32767 / (0.96 * channels)))


def doubled(w_t):
    zero = jnp.zeros_like(w_t)
    return jnp.concatenate(
        [jnp.concatenate([w_t, zero], 1), jnp.concatenate([zero, w_t], 1)], 0
    )


def y_places(blocks, width, lanes, across):
    pieces = [(b, at) for b in range(blocks) for at in range(0, width, lanes)]
    return [(b, at, i // across, i % across * lanes) for i, (b, at) in enumerate(pieces)]


def queries_of(ref):
    return ref.shape[0] * ref.shape[1] * 2


def transition_kernel(
    n_rows,
    pair_hbm, ln_trans_hbm, w_in_hbm, w_out_hbm, w_dist_hbm,
    singles_hbm, restype_hbm, table_hbm, ln_single_hbm, w_attn_hbm, w_single_hbm,
    next_ref, emb_ref, y_ref, w_attn_ref, w_single_ref, *rest,
):
    out_refs, rest = rest[:n_rows], rest[n_rows:]
    (proj_s, pair_s, ln_trans_s, w_in_s, w_out_s, w_dist_s,
     singles_s, restype_s, table_s, ln_single_s, sems) = rest
    blocks, _, groups, length, lanes = proj_s.shape
    keys = groups * length
    tile = length * keys
    moves = [
        pltpu.make_async_copy(source, target, sems.at[i])
        for i, (source, target) in enumerate((
            (restype_hbm, restype_s), (table_hbm, table_s), (singles_hbm, singles_s),
            (ln_single_hbm, ln_single_s), (ln_trans_hbm, ln_trans_s), (pair_hbm, pair_s),
            (w_in_hbm, w_in_s), (w_out_hbm, w_out_s), (w_dist_hbm, w_dist_s),
        ))
    ]
    for move in moves:
        move.start()
    for move in moves[:4]:
        move.wait()
    row = lax.axis_index("rows")
    types = lax.broadcasted_iota(jnp.int32, (table_s.shape[0], restype_s.shape[1]), 0)
    one_hot = (types == restype_s[...]).astype(F32)
    emb = singles_s[...] + lax.dot_general(
        one_hot, table_s[...], TN, precision=lax.Precision.HIGHEST, preferred_element_type=F32
    )
    emb_ref[...] = emb
    gain = jnp.concatenate(
        [ln_single_s[i : i + 1, :] for i in range(ln_single_s.shape[0])], 1
    )
    y = layer_norm(emb, gain).astype(BF16)
    y_ref[...] = y
    for move in moves[4:]:
        move.wait()
    later = [
        pltpu.make_async_copy(w_attn_hbm, w_attn_ref, sems.at[len(moves)]),
        pltpu.make_async_copy(w_single_hbm, w_single_ref, sems.at[len(moves) + 1]),
    ]
    for move in later:
        move.start()
    hidden = w_out_s.shape[0]
    w_dist2 = doubled(w_dist_s[...])
    w_in_s[:, :hidden] = w_in_s[:, :hidden] * jnp.asarray(0.5, BF16)
    span = 4
    count = queries_of(proj_s) // span

    def open_tile(b):
        z = pair_s[b * span * keys : (b + 1) * span * keys, :]
        xt = layer_norm(z, ln_trans_s[...]).astype(BF16)
        return jnp.dot(xt, w_in_s[...], preferred_element_type=F32)

    def gated(gu):
        half, up = gu[:, :hidden], gu[:, hidden:]
        return ((half + half * jnp.tanh(half)) * up).astype(BF16)

    def close_tile(b, hid):
        at = slice(b * span * keys, (b + 1) * span * keys)
        new = pair_s[at, :] + jnp.dot(hid, w_out_s[...], preferred_element_type=F32)
        next_ref[at, :] = new
        return new.astype(BF16)

    def project(b, low):
        pairs = [
            jnp.concatenate(
                [low[t * keys : (t + 1) * keys], low[(t + 1) * keys : (t + 2) * keys]], 1
            )
            for t in range(0, span, 2)
        ]
        proj = lax.dot_general(jnp.concatenate(pairs, 0), w_dist2, NT, preferred_element_type=F32)
        proj = proj.reshape(span // 2, groups, length, lanes)
        for t in range(span // 2):
            at = b * (span // 2) + t
            proj_s[at // (length // 2), at % (length // 2)] = proj[t]

    gus, lows = {0: open_tile(0)}, {}
    for b in range(count):
        if b + 1 < count:
            gus[b + 1] = open_tile(b + 1)
        lows[b] = close_tile(b, gated(gus.pop(b)))
    for b in range(count):
        project(b, lows.pop(b))
    for k in range(n_rows):
        to = row ^ k
        for b in range(blocks):
            for t in range(length // 2):
                out_refs[k][b, :, t * lanes : (t + 1) * lanes] = proj_s[b, t, to].astype(BF16)
        for b, across, group, at in y_places(blocks, y.shape[1], lanes, length // 2):
            out_refs[k][blocks + group, :, at : at + lanes] = y[
                b * length : (b + 1) * length, across : across + lanes
            ]
    for move in later:
        move.wait()


def bias_kernel(next_ref, ln_bias_ref, w_bias_ref, mask_ref, bias_ref):
    heads, channels = w_bias_ref.shape
    blocks, _, groups = mask_ref.shape
    keys, lanes = bias_ref.shape[0], bias_ref.shape[1] // blocks
    length = lanes // heads
    tiled = jnp.concatenate([w_bias_ref[...]] * length, 0)
    owner = lax.broadcasted_iota(jnp.int32, tiled.shape, 0) // heads
    w_big = jnp.concatenate(
        [jnp.where(owner == t, tiled, jnp.zeros_like(tiled)) for t in range(length)], 1
    )
    rows = []
    for b in range(blocks):
        new = next_ref[b * length * keys : (b + 1) * length * keys, :]
        xb = layer_norm(new, ln_bias_ref[...]).astype(BF16)
        rows.append(
            jnp.concatenate([xb[t * keys : (t + 1) * keys] for t in range(length)], 1)
        )
    bias = lax.dot_general(jnp.concatenate(rows, 0), w_big, NT, preferred_element_type=F32)
    for b in range(blocks):
        for a in range(groups):
            keep = jnp.broadcast_to(mask_ref[b, :, a : a + 1], (length, lanes)) > 0
            piece = bias[b * keys + a * length : b * keys + (a + 1) * length]
            coded = jnp.where(keep, jnp.round(piece * bias_scale(channels)), HIDDEN).astype(jnp.int32)
            bias_ref[a * length : (a + 1) * length, b * lanes : (b + 1) * lanes] = coded.astype(
                jnp.int16
            )


def repack_kernel(n_rows, n_cols, *refs):
    got_refs, out_refs = refs[:n_rows][::-1], refs[n_rows:]
    col = lax.axis_index("cols")
    for k in range(n_cols):
        to = pick(ring_step(n_cols, k), col)
        for j in range(n_rows):
            out_refs[k][j] = got_refs[j][to]


def own_kernel(next_ref, w_dist_ref, dist_bias_ref, _, own_ref):
    groups, blocks, length, wide = own_ref.shape
    keys, queries = groups * length, blocks * length
    bins = w_dist_ref.shape[0]
    w_dist2 = doubled(w_dist_ref[...])
    both = jnp.concatenate([dist_bias_ref[...]] * 2, 1)
    for a in range(groups):
        picked = []
        for t in range(0, length, 2):
            halves = [
                next_ref[pl.ds(a * length + t + s, queries, stride=keys), :].astype(BF16)
                for s in range(2)
            ]
            picked.append(jnp.concatenate(halves, 1))
        proj = lax.dot_general(jnp.concatenate(picked, 0), w_dist2, NT, preferred_element_type=F32)
        proj = proj.astype(BF16).astype(F32) + both
        for t in range(length // 2):
            own_ref[a, :, :, t * 2 * bins : (t + 1) * 2 * bins] = proj[
                t * queries : (t + 1) * queries
            ].reshape(blocks, length, 2 * bins)


def attention_kernel(
    n_rows, n_cols, order, heads, scale, next_ref, y_ref, emb_ref, w_attn_ref, w_out_ref, *rest
):
    got_refs, rest = rest[:n_rows][::-1], rest[n_rows:]
    bias_refs, (_, singles_ref, next_hbm, y_s, bias_s, sem) = rest[:n_cols], rest[n_cols:]
    move = pltpu.make_async_copy(next_ref, next_hbm, sem)
    move.start()
    row, col = lax.axis_index("rows"), lax.axis_index("cols")
    blocks, groups, length, width = y_s.shape
    queries = y_ref.shape[0]
    keys = blocks * groups * length
    wide = got_refs[0].shape[2]
    for k in range(n_rows):
        for b, across, group, at in y_places(blocks, width, 128, wide // 128):
            y_s[b, row ^ k, :, across : across + 128] = got_refs[k][
                blocks + group, :, at : at + 128
            ].astype(F32)
    for k in range(n_cols):
        bias_s[pick(ring_step(n_cols, n_cols - k), col)] = bias_refs[order.index(k)][...].astype(jnp.int32).astype(F32)
    y = y_s[...].reshape(keys, width).astype(BF16)
    kv = jnp.dot(y, w_attn_ref[:, width : 3 * width], preferred_element_type=F32).astype(BF16)
    q = jnp.dot(y_ref[...], w_attn_ref[:, :width], preferred_element_type=F32)
    q = (q * (width // heads) ** (-0.5)).astype(BF16)
    gate = sigmoid(jnp.dot(y_ref[...], w_attn_ref[:, 3 * width :], preferred_element_type=F32))
    mine = head_mask(heads, width)
    spread = jnp.where(mine[None], q.astype(F32)[:, None, :], 0.0)
    spread = spread.reshape(queries * heads, width).astype(BF16)
    scores = lax.dot_general(kv[:, :width], spread, NT, preferred_element_type=F32)
    bias = bias_s[...].reshape(keys, queries * heads)
    scores = jnp.where(bias > HIDDEN, scores + bias * (1.0 / scale), MASKED)
    expo = jnp.exp(scores - jnp.max(scores, axis=0, keepdims=True))
    total = jnp.sum(expo, axis=0, keepdims=True)
    acc = lax.dot_general(expo.astype(BF16), kv[:, width:], TN, preferred_element_type=F32)
    total = jnp.transpose(jnp.broadcast_to(total, (8, queries * heads)))[:, :1]
    acc = (acc / total).reshape(queries, heads, width)
    mixed = jnp.sum(jnp.where(mine[None], acc, 0.0), axis=1)
    att = (gate * mixed).astype(BF16)
    singles_ref[...] = emb_ref[...] + jnp.dot(att, w_out_ref[...], preferred_element_type=F32)
    move.wait()


def logit_rows(n_rows, n_cols, steps, own_ref, got_refs, logits_hbm, logits_s, sems):
    row, col = lax.axis_index("rows"), lax.axis_index("cols")
    groups, _, length, _ = own_ref.shape
    moves = []
    for k, got_ref in zip(steps, got_refs):
        source = pick(ring_step(n_cols, n_cols - k), col)
        rows = pl.ds(source * length, length)
        for a in range(groups):
            logits_s[rows, a, :] = own_ref[a, source] + got_ref[row ^ a].astype(F32)
        moves.append(
            pltpu.make_async_copy(logits_s.at[rows], logits_hbm.at[rows], sems.at[k])
        )
        moves[-1].start()
    return moves


def early_kernel(n_rows, n_cols, steps, own_ref, singles_ref, *rest):
    got_refs, (singles_hbm, logits_hbm, logits_s, sems) = rest[: len(steps)], rest[len(steps) :]
    moves = [pltpu.make_async_copy(singles_ref, singles_hbm, sems.at[n_cols])]
    moves[0].start()
    moves += logit_rows(n_rows, n_cols, steps, own_ref, got_refs, logits_hbm, logits_s, sems)
    for move in moves:
        move.wait()


def final_kernel(n_rows, n_cols, steps, own_ref, _, *rest):
    got_refs, (logits_hbm, logits_s, sems) = rest[: len(steps)], rest[len(steps) :]
    for move in logit_rows(
        n_rows, n_cols, steps, own_ref, got_refs, logits_hbm, logits_s, sems
    ):
        move.wait()


def call(kernel, name, outs, scratch, flops, limit, *args, hbm_in=(), hbm_out=(), alias={}):
    shapes = [jax.ShapeDtypeStruct(s, d) for s, d in outs]
    touched = sum(a.size * a.dtype.itemsize for a in (*args, *shapes))
    near = pl.BlockSpec(memory_space=pltpu.VMEM)
    far = pl.BlockSpec(memory_space=pltpu.HBM)
    return pl.pallas_call(
        kernel,
        name=name,
        out_shape=shapes,
        in_specs=[far if i in hbm_in else near for i in range(len(args))],
        out_specs=[far if i in hbm_out else near for i in range(len(shapes))],
        scratch_shapes=scratch,
        input_output_aliases=alias,
        cost_estimate=pl.CostEstimate(flops=flops, bytes_accessed=touched, transcendentals=0),
        compiler_params=pltpu.CompilerParams(vmem_limit_bytes=limit),
    )(*args)


def ring_step(size, step):
    ring = [0, *range(1, size, 2), *reversed(range(2, size, 2))]
    return [ring[(ring.index(i) + step) % size] for i in range(size)]


def pick(table, index):
    return sum(jnp.where(index == i, v, 0) for i, v in enumerate(table))


def exchange_line(values, axis):
    size = len(values)
    return [values[0]] + [
        lax.ppermute(values[k], axis, list(enumerate(ring_step(size, k)))) for k in range(1, size)
    ]


def exchange(values, axis):
    size = len(values)
    return [values[0]] + [
        lax.ppermute(values[k], axis, [(i, i ^ k) for i in range(size)]) for k in range(1, size)
    ]


def local(
    n_rows, n_cols,
    pair, singles, restype, block_mask, ln_trans, w_trans_in, w_trans_out, ln_bias, w_bias,
    restype_table, ln_single, w_attn, w_single_out, w_dist, dist_bias,
):
    queries, groups, length, channels = pair.shape
    keys = groups * length
    blocks = queries // length
    heads = w_bias.shape[1]
    width = w_single_out.shape[0]
    bins = w_dist.shape[1]
    hidden = w_trans_out.shape[0]
    wide = length * bins
    rows = queries * keys
    mib = 1 << 20
    room = (16 if rows <= 2048 else 40) * mib
    inputs = [pltpu.with_memory_space_constraint(a, pltpu.HBM) for a in (
        pair.reshape(rows, channels), ln_trans[None], w_trans_in, w_trans_out, w_dist.T,
        singles, restype[None], restype_table, ln_single.reshape(-1, 128), w_attn, w_single_out,
    )]
    y_groups = -(-blocks * (width // (2 * bins)) // (length // 2))
    first = call(
        functools.partial(transition_kernel, n_rows),
        "transition",
        [
            ((rows, channels), F32),
            ((queries, width), F32),
            ((queries, width), BF16),
            (w_attn.shape, BF16),
            (w_single_out.shape, BF16),
        ]
        + [((blocks + y_groups, length, wide), BF16)] * n_rows,
        [
            pltpu.VMEM((blocks, length // 2, groups, length, 2 * bins), F32),
            *[pltpu.VMEM(a.shape, a.dtype) for a in inputs[:-2]],
            pltpu.SemaphoreType.DMA((len(inputs),)),
        ],
        2 * rows * channels * hidden * 3,
        room,
        *inputs,
        hbm_in=range(len(inputs)),
    )
    pair_next, emb, y, w_attn_near, w_single_near, *blocks_out = first
    got = exchange(blocks_out, "rows")
    (bias,) = call(
        bias_kernel,
        "bias",
        [((keys, queries * heads), jnp.int16)],
        [],
        2 * rows * channels * 1024,
        room,
        pair_next, ln_bias[None], w_bias.T, jnp.transpose(block_mask, (0, 2, 1)),
    )
    order = [n_cols // 2] + [k for k in range(1, n_cols) if k != n_cols // 2] + [0]
    order_m = [*range(1, n_cols), 0]
    biases = exchange_line([bias] * n_cols, "cols")
    outgoing = call(
        functools.partial(repack_kernel, n_rows, n_cols),
        "repack",
        [((groups, length, wide), BF16)] * n_cols,
        [],
        2 * rows * channels * 64,
        room,
        *got[::-1],
    )
    mirrored = exchange_line(outgoing, "cols")
    (own,) = call(
        own_kernel,
        "own",
        [((groups, blocks, length, wide), F32)],
        [],
        2 * rows * channels * 1024,
        room,
        pair_next, w_dist.T, dist_bias[None], outgoing[0],
    )
    singles_near, pair_out = call(
        functools.partial(attention_kernel, n_rows, n_cols, order, heads, bias_scale(channels)),
        "attention",
        [((queries, width), F32), ((rows, channels), F32)],
        [
            pltpu.VMEM((blocks, groups, length, width), F32),
            pltpu.VMEM((n_cols, keys, queries * heads), F32),
            pltpu.SemaphoreType.DMA,
        ],
        2 * rows * channels * 1024,
        room,
        pair_next, y, emb, w_attn_near, w_single_near,
        *got[::-1], *[biases[k] for k in order], own,
        hbm_out=(1,),
    )
    last = [
        pltpu.VMEM((queries, groups, wide), F32),
        pltpu.SemaphoreType.DMA((n_cols + 1,)),
    ]
    soon, late = [0, *order_m[:1]], order_m[1:-1]
    singles_next, dist_logits = call(
        functools.partial(early_kernel, n_rows, n_cols, soon),
        "early",
        [((queries, width), F32), ((queries, groups, wide), F32)],
        last,
        2 * rows * channels * 64,
        room,
        own, singles_near, *[mirrored[k] for k in soon],
        hbm_out=(0, 1),
    )
    (dist_logits,) = call(
        functools.partial(final_kernel, n_rows, n_cols, late),
        "final",
        [((queries, groups, wide), F32)],
        last,
        2 * rows * channels * 64,
        room,
        own, dist_logits, *[mirrored[k] for k in late],
        hbm_in=(1,),
        hbm_out=(0,),
        alias={1: 0},
    )
    return pair_out.reshape(pair.shape), singles_next, dist_logits


def solution(mesh):
    return jax.shard_map(
        functools.partial(local, mesh.shape["rows"], mesh.shape["cols"]),
        mesh=mesh,
        in_specs=(
            P(("parts", "rows"), None, "cols", None),
            P(("parts", "rows"), None),
            P(("parts", "rows")),
            P(("parts", "rows"), None, "cols"),
            *([P()] * 11),
        ),
        out_specs=(
            P(("parts", "rows"), None, "cols", None),
            P(("parts", "rows"), None),
            P(("parts", "rows"), None, "cols"),
        ),
        check_vma=False,
    )
```
